32 devices in a mesh: scen: 8 (over y, x, core), col: 4 (over z).
Axes of the slice: x: 2, y: 2, z: 4, core: 2. Of those that a mesh axis runs over, the one named last changes fastest.
Arguments:
- inverses: float32 [8, 1024, 1024], P('scen'), as said below
- coupling: float32 [8, 1024, 4096], P('scen', None, 'col'), may hold values from -0.1875 to 0.1875
- tile_mask: int32 [8, 8], P('scen'), may hold values 0 or 1
- hess_diag: float32 [512], replicated, may hold values from 1 to 16
Outputs:
- factor: float32 [4096, 512], P(('col', 'scen'))
The draws below stay inside these ranges and needn't reach their ends.
Inputs may be any that keep to these rules, and one draw needn't show every extreme that they name: `inverses`: each scenario's matrix is symmetric and positive definite.
All inputs are finite; a program needn't handle non-finite values. No bound on the sum of `tile_mask` on one device may be relied on, other than what follows from the above.
Results may differ from the reference program's by a relative error of at most 0.0001.
Values sent between devices are 32-bit elements; how exact they have to be, the bound alone decides.
No kernel may reach another device: no remote copies, remote signals or barrier semaphores. Data moves between devices by JAX's collectives and lax.ppermute only.
A program may use at most 64 MiB of HBM per device.

```python
import math
import jax
import jax.numpy as jnp
from jax import lax

NS = 1024
TILE = 128
PW = 256
NT = 8
NF = 4096
SCEN = 8


def draw_inverses(key, part):
    first = jax.random.fold_in(key, 11)
    second = jax.random.fold_in(key, 12)
    diagonal = jax.random.uniform(first, (SCEN, NS), jnp.float32, 1.0, 2.0)
    noise = jax.random.normal(second, (SCEN, NS, NS), jnp.float32)
    noise = noise * (0.3 / NS ** 0.5)
    sym = (noise + jnp.swapaxes(noise, 1, 2)) * 0.5 ** 0.5
    eye = jnp.eye(NS, dtype=jnp.float32)
    return sym + diagonal[:, :, None] * eye[None, :, :]


def set_ends(entries, rng, smallest, largest):
    extent = entries.shape
    index_at = [jax.random.randint(jax.random.fold_in(rng, axis), (), 0, extent[axis]) for axis in range(len(extent))]
    entries = entries.at[tuple(index_at)].set(smallest)
    longest = extent.index(max(extent))
    index_at[longest] = (index_at[longest] + 1) % extent[longest]
    return entries.at[tuple(index_at)].set(largest)


def block_scale(rng, shape, pieces, least, largest):
    loudness = 1.0
    for axis_at, parts in pieces:
        steps = jax.random.uniform(jax.random.fold_in(jax.random.fold_in(rng, 6), axis_at), (parts,), jnp.float32, least / len(pieces), largest / len(pieces))
        loudness = loudness * jnp.repeat(jnp.exp(steps), shape[axis_at] // parts).reshape((-1,) + (1,) * (len(shape) - 1 - axis_at))
    return loudness


def bell_draw(stream_key, extent, deviation, limit, pieces=(), kind=jnp.bfloat16):
    drawn = deviation * jax.random.normal(stream_key, extent, jnp.float32)
    if pieces:
        drawn = drawn * block_scale(stream_key, extent, pieces, -0.22, 0.18)
    return jnp.clip(drawn, -limit, limit).astype(kind)


def setup_inputs(seed: int = 0) -> dict:
    seeds = jax.random.split(jax.random.key(seed), 5)
    inverses = draw_inverses(jax.random.fold_in(seeds[4], 71), 0)
    coupling = bell_draw(seeds[1], (SCEN, NS, NF), NS ** -0.5, 0.1875, ((0, 8), (2, 4)), jnp.float32)
    tile_mask = set_ends((jax.random.randint(seeds[2], (SCEN, NT), 0, 4) < 3).astype(jnp.int32), jax.random.fold_in(seeds[2], 1), 0, 1)
    hess_diag = jnp.clip(jnp.exp(jax.random.uniform(seeds[3], (2 * PW,), jnp.float32, math.log(1.0), math.log(16.0))), 1.0, 16.0)
    return dict(inverses=inverses, coupling=coupling, tile_mask=tile_mask, hess_diag=hess_diag)


def reference(inverses, coupling, tile_mask, hess_diag):
    width = 2 * PW
    highest = lax.Precision.HIGHEST

    def add_one(total, item):
        inverse, block, keep = item
        row_keep = jnp.repeat(keep.astype(jnp.float32), TILE)
        masked = block * row_keep[:, None]
        product = jnp.dot(inverse.astype(jnp.float32), masked[:, :width].astype(jnp.float32), precision=highest, preferred_element_type=jnp.float32)
        contrib = lax.dot_general(masked.astype(jnp.float32), product.astype(jnp.float32), (((0,), (0,)), ((), ())), precision=highest, preferred_element_type=jnp.float32)
        return (total + contrib, None)
    schur, _ = lax.scan(add_one, jnp.zeros((NF, width), jnp.float32), (inverses, coupling, tile_mask))
    diag_index = jnp.arange(width)
    schur = schur.at[diag_index, diag_index].add(hess_diag)
    row_index = jnp.arange(NF)[:, None]
    chol1 = jnp.linalg.cholesky(schur[:PW, :PW])
    inv1 = jax.scipy.linalg.solve_triangular(chol1, jnp.eye(PW, dtype=jnp.float32), lower=True)
    lcol1 = jnp.dot(schur[:, :PW].astype(jnp.float32), inv1.T.astype(jnp.float32), precision=highest, preferred_element_type=jnp.float32)
    padded1 = jnp.concatenate([chol1, jnp.zeros((NF - PW, PW), jnp.float32)], axis=0)
    lcol1 = jnp.where(row_index < PW, padded1, lcol1)
    lower_b = lcol1[PW:width]
    update = schur[PW:width, PW:] - jnp.dot(lower_b.astype(jnp.float32), lower_b.T.astype(jnp.float32), precision=highest, preferred_element_type=jnp.float32)
    chol2 = jnp.linalg.cholesky(update)
    inv2 = jax.scipy.linalg.solve_triangular(chol2, jnp.eye(PW, dtype=jnp.float32), lower=True)
    rest = schur[:, PW:] - jnp.dot(lcol1.astype(jnp.float32), lower_b.T.astype(jnp.float32), precision=highest, preferred_element_type=jnp.float32)
    lcol2 = jnp.dot(rest.astype(jnp.float32), inv2.T.astype(jnp.float32), precision=highest, preferred_element_type=jnp.float32)
    padded2 = jnp.concatenate([jnp.zeros((PW, PW), jnp.float32), chol2, jnp.zeros((NF - width, PW), jnp.float32)], axis=0)
    lcol2 = jnp.where(row_index < width, padded2, lcol2)
    return jnp.concatenate([lcol1, lcol2], axis=1)
```

```python
import functools

import jax
import jax.numpy as jnp
from jax import lax
from jax.experimental import pallas as pl
from jax.experimental.pallas import tpu as pltpu
from jax.sharding import PartitionSpec as P

BLOCK = 128
SUB = 8


def high(left, right, dims):
    return lax.dot_general(
        left, right, (dims, ((), ())), precision=lax.Precision.HIGH, preferred_element_type=jnp.float32
    )


def full(left, right, dims):
    return lax.dot_general(
        left, right, (dims, ((), ())), precision=lax.Precision.HIGHEST, preferred_element_type=jnp.float32
    )


def eliminate(tiles):
    count, size = len(tiles), tiles[0].shape[1]
    lane = lax.broadcasted_iota(jnp.int32, (SUB, size), 1)
    sub = lax.broadcasted_iota(jnp.int32, (SUB, size), 0)

    def lanes(x, c):
        return jnp.broadcast_to(x[:, c : c + 1], (SUB, size))

    def subs(x, q):
        return jnp.broadcast_to(x[q : q + 1, :], (SUB, size))

    scaled, scales = [], []
    for at in range(count):
        low = SUB * at
        rows = tiles[at]
        cols = [lanes(rows, low + q) for q in range(SUB)]
        inverse, upper, pivots = [], {}, None
        for q in range(SUB):
            pivot = subs(cols[q], q)
            pivots = pivot if pivots is None else jnp.where(sub == q, pivot, pivots)
            inverse.append(1.0 / pivot)
            times = jnp.where(sub > q, cols[q] * inverse[q], 0.0)
            for p in range(q + 1, SUB):
                upper[q, p] = subs(cols[q], p)
                cols[p] = cols[p] - times * upper[q, p]
            pivot_row = jnp.where(lane == low + q, 1.0, subs(rows, q))
            rows = jnp.where((lane == low + q) & (sub > q), 0.0, rows) - times * pivot_row
        pivot_rows = []
        for q in range(SUB):
            row = jnp.where(lane == low + q, 1.0, subs(rows, q))
            pivot_rows.append(jnp.where((lane > low + q) & (lane < low + SUB), 0.0, row))
        own = (lane >= low) & (lane < low + SUB)
        for other in range(at + 1, count):
            tile = tiles[other]
            theirs = [lanes(tile, low + q) for q in range(SUB)]
            tile = jnp.where(own, 0.0, tile)
            times = []
            for q in range(SUB):
                value = theirs[q]
                for p in range(q):
                    value = value - times[p] * upper[p, q]
                value = value * inverse[q]
                times.append(value)
                tile = tile - value * pivot_rows[q]
            tiles[other] = tile
        scale = lax.rsqrt(pivots)
        scales.append(scale)
        scaled.append(rows * scale)
    return scaled, scales


def factor_kernel(plane_ref, a_ref, l_ref, w_ref, base_ref, scale_ref):
    size = a_ref.shape[0]

    @pl.when(plane_ref[0] == 0)
    def _():
        w_ref[...] = a_ref[...]

        def step(j, carry):
            low = pl.multiple_of(j * BLOCK, BLOCK)
            mine = pl.ds(low, BLOCK)
            tiles = [w_ref[pl.ds(low + SUB * t, SUB), mine] for t in range(BLOCK // SUB)]
            scaled, scales = eliminate(tiles)
            for t in range(BLOCK // SUB):
                base_ref[SUB * t : SUB * t + SUB, :] = scaled[t]
                scale_ref[SUB * t : SUB * t + SUB, :] = scales[t]
            both = base_ref[...]
            row = lax.broadcasted_iota(jnp.int32, (BLOCK, BLOCK), 0)
            col = lax.broadcasted_iota(jnp.int32, (BLOCK, BLOCK), 1)
            inverse = jnp.where(col < row, both, jnp.where(col == row, scale_ref[...], 0.0))
            factor_t = jnp.where(col >= row, both, 0.0)
            below = lax.broadcasted_iota(jnp.int32, (size, BLOCK), 0) >= low + BLOCK
            panel = jnp.where(below, full(w_ref[:, mine], inverse, ((1,), (1,))), 0.0)
            w_ref[mine, :] = full(inverse, w_ref[mine, :], ((1,), (0,)))
            w_ref[mine, mine] = inverse
            pivot_rows = w_ref[mine, :]
            w_ref[:, mine] = jnp.where(below, 0.0, w_ref[:, mine])
            w_ref[...] = w_ref[...] - full(panel, pivot_rows, ((1,), (0,)))
            l_ref[:, mine] = panel
            l_ref[mine, mine] = factor_t.T
            return carry

        lax.fori_loop(0, size // BLOCK, step, 0)
        row = lax.broadcasted_iota(jnp.int32, (size, size), 0)
        col = lax.broadcasted_iota(jnp.int32, (size, size), 1)
        w_ref[...] = jnp.where(col <= row, w_ref[...], 0.0)


def factor(plane, a):
    size = a.shape[0]
    return pl.pallas_call(
        factor_kernel,
        out_shape=(jax.ShapeDtypeStruct((size, size), jnp.float32),) * 2,
        in_specs=[pl.BlockSpec(memory_space=pltpu.SMEM), pl.BlockSpec(memory_space=pltpu.VMEM)],
        out_specs=(pl.BlockSpec(memory_space=pltpu.VMEM),) * 2,
        scratch_shapes=[pltpu.VMEM((BLOCK, BLOCK), jnp.float32)] * 2,
        cost_estimate=pl.CostEstimate(flops=2 * size**3, bytes_accessed=12 * size * size, transcendentals=size),
    )(plane, a)


def pack(a):
    nb = a.shape[0] // BLOCK
    strips = []
    for i in range(nb // 2):
        k = nb - 1 - i
        strips.append(
            jnp.concatenate(
                [a[k * BLOCK : (k + 1) * BLOCK, : (k + 1) * BLOCK], a[i * BLOCK : (i + 1) * BLOCK, : (i + 1) * BLOCK]],
                axis=1,
            )
        )
    return jnp.concatenate(strips, axis=0)


def unpack(p, nb):
    strips = [None] * nb
    for i in range(nb // 2):
        k = nb - 1 - i
        strip = p[i * BLOCK : (i + 1) * BLOCK]
        for b, low in ((k, 0), (i, (k + 1) * BLOCK)):
            part = strip[:, low : low + (b + 1) * BLOCK]
            strips[b] = jnp.pad(part, ((0, 0), (0, (nb - 1 - b) * BLOCK)))
    return jnp.concatenate(strips, axis=0)


def exchange(x, bit, count):
    return lax.ppermute(x, "scen", [(i, i ^ (1 << bit)) for i in range(count)])


def orders(count):
    bits = count.bit_length() - 1
    split = 1 + (bits - 1 + 1) // 2
    near, first, second = [0], list(range(1, split)), list(range(split, bits))
    return bits, near, first, second


def halve(x, names, bit, count):
    axis = names.index(bit)
    mine = (lax.axis_index("scen") >> bit) & 1
    keep = lax.dynamic_index_in_dim(x, mine, axis, keepdims=False)
    send = lax.dynamic_index_in_dim(x, 1 - mine, axis, keepdims=False)
    return keep + exchange(send, bit, count), [n for n in names if n != bit]


def scatter_sum(x):
    count = lax.axis_size("scen")
    bits, near, first, second = orders(count)
    rows = x.shape[0] // count
    x = x.reshape((2,) * bits + (rows,) + x.shape[1:])
    names = list(range(bits - 1, -1, -1))
    for bit in near:
        x, names = halve(x, names, bit, count)
    lead = (slice(None),) * len(names)
    parts = [x[lead + (slice(0, rows // 2),)], x[lead + (slice(rows // 2, rows),)]]
    lists = [list(names), list(names)]
    for a, b in zip(first + second, second + first):
        for i, bit in ((0, a), (1, b)):
            parts[i], lists[i] = halve(parts[i], lists[i], bit, count)
    return jnp.concatenate(parts, axis=0)


def gather_rows(x):
    count = lax.axis_size("scen")
    bits, near, first, second = orders(count)
    rows = x.shape[0]
    me = lax.axis_index("scen")

    def grow(part, names, bit):
        other = exchange(part, bit, count)
        low = ((me >> bit) & 1) == 0
        names2 = sorted(names + [bit], reverse=True)
        pair = [jnp.where(low, part, other), jnp.where(low, other, part)]
        return jnp.stack(pair, axis=names2.index(bit)), names2

    parts, lists = [x[: rows // 2], x[rows // 2 :]], [[], []]
    for a, b in zip((first + second)[::-1], (second + first)[::-1]):
        for i, bit in ((0, a), (1, b)):
            parts[i], lists[i] = grow(parts[i], lists[i], bit)
    whole, names = jnp.concatenate(parts, axis=len(lists[0])), lists[0]
    for bit in near[::-1]:
        whole, names = grow(whole, names, bit)
    return whole.reshape((count * rows,) + x.shape[1:])


def body(inverses, coupling, tile_mask, hess_diag):
    local = coupling[0]
    width = hess_diag.shape[0]
    nb = width // BLOCK
    scen, cols = lax.axis_size("scen"), lax.axis_size("col")
    me, plane = lax.axis_index("scen"), lax.axis_index("col")
    rows = local.shape[1] // scen
    keep = jnp.repeat(tile_mask[0].astype(jnp.float32), local.shape[0] // tile_mask.shape[1])
    masked_inverse = inverses[0] * keep[:, None] * keep[None, :]
    halves, quarters = 2, 4
    half = width // halves
    quarter = local.shape[0] // quarters

    products = [high(masked_inverse, local[:, h * half : (h + 1) * half], ((1,), (0,))) for h in range(halves)]

    chunks = []
    for h in range(halves):
        for q in range(quarters):
            piece = products[h][q * quarter : (q + 1) * quarter]
            mine = jnp.where(plane == 0, piece, 0.0)
            for hop in range(cols - 1):
                piece = lax.ppermute(piece, "col", [(hop, hop + 1)])
                mine = mine + piece
            chunks.append(mine)

    product = jnp.concatenate(products, axis=1)
    corner = high(local[:, :width], product, ((0,), (0,)))
    packed = gather_rows(scatter_sum(pack(corner)))
    square = unpack(packed, nb)
    square = jnp.tril(square)
    square = square + jnp.tril(square, -1).T + jnp.diag(hess_diag)
    lower, winv = factor(plane.astype(jnp.int32).reshape(1), square)

    packed = pack(winv)
    each = packed.shape[0] // scen
    part = lax.dynamic_slice_in_dim(packed, me * each, each, 0)
    sent = jnp.where(plane == 0, part, 0.0)
    for hop in range(1, cols):
        sent = sent + lax.ppermute(part, "col", [(0, hop)])
    winv = unpack(gather_rows(sent), nb)

    sums = []
    for h in range(halves):
        whole = jnp.concatenate(chunks[h * quarters : (h + 1) * quarters], axis=0)
        sums.append(scatter_sum(high(local, whole, ((0,), (0,)))))
    solved = full(jnp.concatenate(sums, axis=1), winv, ((1,), (1,)))
    first = plane * local.shape[1] + me * rows
    own = lax.dynamic_slice_in_dim(lower, jnp.clip(first, 0, width - rows), rows, 0)
    return jnp.where(first < width, own, solved)


def solution(mesh):
    in_specs = (P("scen", None, None), P("scen", None, "col"), P("scen", None), P())
    out_specs = P(("col", "scen"), None)
    return jax.shard_map(body, mesh=mesh, in_specs=in_specs, out_specs=out_specs, check_vma=False)
```

```python
import functools

import jax
import jax.numpy as jnp
from jax import lax
from jax.experimental import pallas as pl
from jax.experimental.pallas import tpu as pltpu
from jax.sharding import PartitionSpec as P


BLOCK = 128
SUB = 8


def high(left, right, dims):
    return lax.dot_general(
        left, right, (dims, ((), ())), precision=lax.Precision.HIGH, preferred_element_type=jnp.float32
    )


def full(left, right, dims):
    return lax.dot_general(
        left, right, (dims, ((), ())), precision=lax.Precision.HIGHEST, preferred_element_type=jnp.float32
    )


def eliminate(tiles):
    count, size = len(tiles), tiles[0].shape[1]
    lane = lax.broadcasted_iota(jnp.int32, (SUB, size), 1)
    sub = lax.broadcasted_iota(jnp.int32, (SUB, size), 0)

    def lanes(x, c):
        return jnp.broadcast_to(x[:, c : c + 1], (SUB, size))

    def subs(x, q):
        return jnp.broadcast_to(x[q : q + 1, :], (SUB, size))

    scaled, scales = [], []
    for at in range(count):
        low = SUB * at
        rows = tiles[at]
        cols = [lanes(rows, low + q) for q in range(SUB)]
        inverse, upper, pivots = [], {}, None
        for q in range(SUB):
            pivot = subs(cols[q], q)
            pivots = pivot if pivots is None else jnp.where(sub == q, pivot, pivots)
            inverse.append(1.0 / pivot)
            times = jnp.where(sub > q, cols[q] * inverse[q], 0.0)
            for p in range(q + 1, SUB):
                upper[q, p] = subs(cols[q], p)
                cols[p] = cols[p] - times * upper[q, p]
            pivot_row = jnp.where(lane == low + q, 1.0, subs(rows, q))
            rows = jnp.where((lane == low + q) & (sub > q), 0.0, rows) - times * pivot_row
        pivot_rows = []
        for q in range(SUB):
            row = jnp.where(lane == low + q, 1.0, subs(rows, q))
            pivot_rows.append(jnp.where((lane > low + q) & (lane < low + SUB), 0.0, row))
        own = (lane >= low) & (lane < low + SUB)
        for other in range(at + 1, count):
            tile = tiles[other]
            theirs = [lanes(tile, low + q) for q in range(SUB)]
            tile = jnp.where(own, 0.0, tile)
            times = []
            for q in range(SUB):
                value = theirs[q]
                for p in range(q):
                    value = value - times[p] * upper[p, q]
                value = value * inverse[q]
                times.append(value)
                tile = tile - value * pivot_rows[q]
            tiles[other] = tile
        scale = lax.rsqrt(pivots)
        scales.append(scale)
        scaled.append(rows * scale)
    return scaled, scales


def vmem(count):
    return [pl.BlockSpec(memory_space=pltpu.VMEM)] * count


SMEM = pl.BlockSpec(memory_space=pltpu.SMEM)


def shape(*sizes):
    return jax.ShapeDtypeStruct(sizes, jnp.float32)


def strips(nb):
    for i in range(nb // 2):
        yield i, nb - 1 - i, 0
        yield i, i, (nb - i) * BLOCK


def pack_kernel(core_ref, corner_ref, keep_a_ref, keep_b_ref, send_ref, rect_ref):
    nb = corner_ref.shape[0] // BLOCK
    for i, block, low in strips(nb):
        wide = (block + 1) * BLOCK
        rect_ref[i * BLOCK : (i + 1) * BLOCK, low : low + wide] = corner_ref[
            block * BLOCK : (block + 1) * BLOCK, :wide
        ]
    half = rect_ref.shape[0] // 2
    core = core_ref[0]
    mine = pl.multiple_of(core * half, half)
    theirs = pl.multiple_of((1 - core) * half, half)
    keep_a_ref[...] = rect_ref[pl.ds(mine, half // 2), :]
    keep_b_ref[...] = rect_ref[pl.ds(mine + half // 2, half // 2), :]
    send_ref[...] = rect_ref[pl.ds(theirs, half), :]


def pack(core, corner):
    nb = corner.shape[0] // BLOCK
    tall, wide = nb // 2 * BLOCK, (nb + 1) * BLOCK
    return pl.pallas_call(
        pack_kernel,
        out_shape=(shape(tall // 4, wide), shape(tall // 4, wide), shape(tall // 2, wide)),
        in_specs=[SMEM] + vmem(1),
        out_specs=tuple(vmem(3)),
        scratch_shapes=[pltpu.VMEM((tall, wide), jnp.float32)],
        cost_estimate=pl.CostEstimate(flops=0, bytes_accessed=8 * tall * wide, transcendentals=0),
    )(core, corner)


def factor_kernel(place_ref, own_a, own_b, other_a, other_b, diag_ref, l_ref, piece_ref, w_ref, rect_ref, base_ref, scale_ref):
    size = w_ref.shape[0]
    nb = size // BLOCK
    plane, me = place_ref[0], place_ref[1]

    @pl.when(plane == 0)
    def _():
        half = rect_ref.shape[0] // 2
        quarter = half // 2
        core = me & 1
        mine = pl.multiple_of(core * half, half)
        theirs = pl.multiple_of((1 - core) * half, half)
        rect_ref[pl.ds(mine, quarter), :] = own_a[...]
        rect_ref[pl.ds(mine + quarter, quarter), :] = own_b[...]
        rect_ref[pl.ds(theirs, quarter), :] = other_a[...]
        rect_ref[pl.ds(theirs + quarter, quarter), :] = other_b[...]
        row = lax.broadcasted_iota(jnp.int32, (BLOCK, BLOCK), 0)
        col = lax.broadcasted_iota(jnp.int32, (BLOCK, BLOCK), 1)
        for i, block, low in strips(nb):
            here = slice(block * BLOCK, (block + 1) * BLOCK)
            for k in range(block + 1):
                there = slice(k * BLOCK, (k + 1) * BLOCK)
                part = rect_ref[i * BLOCK : (i + 1) * BLOCK, low + k * BLOCK : low + (k + 1) * BLOCK]
                if k == block:
                    part = jnp.where(col <= row, part, part.T)
                    part = part + jnp.where(col == row, diag_ref[:, here], 0.0)
                else:
                    w_ref[there, here] = part.T
                w_ref[here, there] = part

        def step(j, carry):
            low = pl.multiple_of(j * BLOCK, BLOCK)
            mine = pl.ds(low, BLOCK)
            tiles = [w_ref[pl.ds(low + SUB * t, SUB), mine] for t in range(BLOCK // SUB)]
            scaled, scales = eliminate(tiles)
            for t in range(BLOCK // SUB):
                base_ref[SUB * t : SUB * t + SUB, :] = scaled[t]
                scale_ref[SUB * t : SUB * t + SUB, :] = scales[t]
            both = base_ref[...]
            inverse = jnp.where(col < row, both, jnp.where(col == row, scale_ref[...], 0.0))
            factor_t = jnp.where(col >= row, both, 0.0)
            below = lax.broadcasted_iota(jnp.int32, (size, BLOCK), 0) >= low + BLOCK
            panel = jnp.where(below, full(w_ref[:, mine], inverse, ((1,), (1,))), 0.0)
            w_ref[mine, :] = full(inverse, w_ref[mine, :], ((1,), (0,)))
            w_ref[mine, mine] = inverse
            pivot_rows = w_ref[mine, :]
            w_ref[:, mine] = jnp.where(below, 0.0, w_ref[:, mine])
            w_ref[...] = w_ref[...] - full(panel, pivot_rows, ((1,), (0,)))
            l_ref[:, mine] = panel
            l_ref[mine, mine] = factor_t.T
            return carry

        lax.fori_loop(0, nb, step, 0)
        for i, block, low in strips(nb):
            for k in range(block + 1):
                rect_ref[i * BLOCK : (i + 1) * BLOCK, low + k * BLOCK : low + (k + 1) * BLOCK] = w_ref[
                    block * BLOCK : (block + 1) * BLOCK, k * BLOCK : (k + 1) * BLOCK
                ]
        each = piece_ref.shape[0]
        piece_ref[...] = rect_ref[pl.ds(pl.multiple_of(me * each, each), each), :]


def factor(place, parts, diag, each):
    size = diag.shape[1]
    nb = size // BLOCK
    tall, wide = nb // 2 * BLOCK, (nb + 1) * BLOCK
    return pl.pallas_call(
        factor_kernel,
        out_shape=(shape(size, size), shape(each, wide)),
        in_specs=[SMEM] + vmem(5),
        out_specs=tuple(vmem(2)),
        scratch_shapes=[
            pltpu.VMEM((size, size), jnp.float32),
            pltpu.VMEM((tall, wide), jnp.float32),
            pltpu.VMEM((BLOCK, BLOCK), jnp.float32),
            pltpu.VMEM((BLOCK, BLOCK), jnp.float32),
        ],
        cost_estimate=pl.CostEstimate(flops=20 * size**3, bytes_accessed=12 * size * size, transcendentals=size),
    )(place, *parts, diag)


def last_kernel(count, place_ref, *refs):
    pieces, (keep_a, got_a, keep_b, got_b, l_ref, out_ref, rect_ref, rows_ref) = refs[:count], refs[count:]
    me, first = place_ref[1], place_ref[2]
    rows, width = out_ref.shape
    nb = width // BLOCK
    each = pieces[0].shape[0]
    half = rows // 2
    rows_ref[:half, :] = keep_a[...] + got_a[...]
    rows_ref[half:, :] = keep_b[...] + got_b[...]
    for m in range(count):
        rect_ref[pl.ds(pl.multiple_of((me ^ m) * each, each), each), :] = pieces[m][...]
    for i, block, low in strips(nb):
        wide = (block + 1) * BLOCK
        part = rect_ref[i * BLOCK : (i + 1) * BLOCK, low : low + wide]
        part = jnp.concatenate(
            [part[:, : wide - BLOCK], jnp.where(
                lax.broadcasted_iota(jnp.int32, (BLOCK, BLOCK), 1) <= lax.broadcasted_iota(jnp.int32, (BLOCK, BLOCK), 0),
                part[:, wide - BLOCK :], 0.0)], axis=1) if wide > BLOCK else part
        out_ref[:, block * BLOCK : (block + 1) * BLOCK] = full(rows_ref[:, :wide], part, ((1,), (1,)))

    @pl.when(first < width)
    def _():
        out_ref[...] = l_ref[pl.ds(pl.multiple_of(first, rows), rows), :]


def last(place, pieces, sums, lower, rows):
    width = lower.shape[0]
    nb = width // BLOCK
    tall, wide = nb // 2 * BLOCK, (nb + 1) * BLOCK
    return pl.pallas_call(
        functools.partial(last_kernel, len(pieces)),
        out_shape=shape(rows, width),
        in_specs=[SMEM] + vmem(len(pieces) + 5),
        out_specs=vmem(1)[0],
        scratch_shapes=[pltpu.VMEM((tall, wide), jnp.float32), pltpu.VMEM((rows, width), jnp.float32)],
        cost_estimate=pl.CostEstimate(flops=6 * rows * width * width, bytes_accessed=8 * width * width, transcendentals=0),
    )(place, *pieces, *sums, lower)


def hop(x, source, target):
    return lax.ppermute(x, "col", [(source, target)])


def exchange(x, mask, count):
    return lax.ppermute(x, "scen", [(i, i ^ mask) for i in range(count)])


def orders(count):
    bits = count.bit_length() - 1
    split = 1 + bits // 2
    return bits, list(range(1, split)), list(range(split, bits))


def halve(x, names, bit, count):
    axis = names.index(bit)
    mine = (lax.axis_index("scen") >> bit) & 1
    keep = lax.dynamic_index_in_dim(x, mine, axis, keepdims=False)
    send = lax.dynamic_index_in_dim(x, 1 - mine, axis, keepdims=False)
    return keep, exchange(send, 1 << bit, count), [n for n in names if n != bit]


def scatter_sum(x):
    count = lax.axis_size("scen")
    bits, first, second = orders(count)
    rows = x.shape[0] // count
    x = x.reshape((2,) * bits + (rows,) + x.shape[1:])
    keep, got, names = halve(x, list(range(bits - 1, -1, -1)), 0, count)
    x = keep + got
    lead = (slice(None),) * len(names)
    parts = [x[lead + (slice(0, rows // 2),)], x[lead + (slice(rows // 2, rows),)]]
    lists, pairs = [names, names], [None, None]
    for a, b in zip(first + second, second + first):
        for i, bit in ((0, a), (1, b)):
            if pairs[i] is not None:
                parts[i] = pairs[i][0] + pairs[i][1]
            keep, got, lists[i] = halve(parts[i], lists[i], bit, count)
            pairs[i] = (keep, got)
    return pairs[0] + pairs[1]


PIECES = 8
HEAD = 2
LATE = 2


def bounds(depth):
    units = depth // SUB
    return [units * k // PIECES * SUB for k in range(PIECES + 1)]


def program(inverses, coupling, tile_mask, hess_diag):
    local = coupling[0]
    width = hess_diag.shape[0]
    scen, planes = lax.axis_size("scen"), lax.axis_size("col")
    me, plane = lax.axis_index("scen").astype(jnp.int32), lax.axis_index("col").astype(jnp.int32)
    rows = local.shape[1] // scen
    first = plane * local.shape[1] + me * rows
    place = jnp.stack([plane, me, first])
    depth = local.shape[0]
    keep = jnp.repeat(tile_mask[0].astype(jnp.float32), depth // tile_mask.shape[1])
    masked_inverse = inverses[0] * keep[:, None] * keep[None, :]
    panel = local[:, :width]
    edge = bounds(depth)

    cut = edge[HEAD]
    head = high(masked_inverse[:cut], panel, ((1,), (0,)))
    tail = high(masked_inverse[cut:], panel, ((1,), (0,)))

    heads = lax.optimization_barrier(tuple(head[edge[k] : edge[k + 1]] for k in range(HEAD)))
    tails = lax.optimization_barrier(tuple(tail[edge[k] - cut : edge[k + 1] - cut] for k in range(HEAD, PIECES)))
    arrived = []
    for k in range(PIECES):
        piece = (heads + tails)[k]
        mine = jnp.where(plane == 0, piece, 0.0)
        for h in range(planes - 1):
            piece = hop(piece, h, h + 1)
            mine = mine + piece
        arrived.append(mine)

    corner = high(panel[:cut], head, ((0,), (0,))) + high(panel[cut:], tail, ((0,), (0,)))
    keep_a, keep_b, send = pack((me & 1).reshape(1), corner)
    got = exchange(send, 1, scen)
    a, b = keep_a + got[: got.shape[0] // 2], keep_b + got[got.shape[0] // 2 :]
    _, near, far = orders(scen)
    for p, q in zip(near + far, far + near):
        got_a = exchange(a, 1 << p, scen)
        got_b = exchange(b, 1 << q, scen)
        a, b = a + got_a, b + got_b
    parts = (a, b, exchange(a, 1, scen), exchange(b, 1, scen))
    each = width // BLOCK // 2 * BLOCK // scen
    lower, piece = factor(place, parts, hess_diag[None, :], each)

    mine = jnp.where(plane == 0, piece, 0.0)
    for h in range(1, planes):
        mine = mine + hop(piece, 0, h)
    pieces = [mine if m == 0 else exchange(mine, m, scen) for m in range(0, scen, 2)]
    pieces = [p for m in range(0, scen, 2) for p in (pieces[m // 2], exchange(pieces[m // 2], 1, scen))]

    early = edge[PIECES - LATE]
    top = jnp.concatenate(arrived[: PIECES - LATE], axis=0)
    bottom = jnp.concatenate(arrived[PIECES - LATE :], axis=0)
    total = high(local[:early], top, ((0,), (0,)))
    total = total + high(local[early:], bottom, ((0,), (0,)))
    return last(place, pieces, scatter_sum(total), lower, rows)


def solution(mesh):
    in_specs = (P("scen", None, None), P("scen", None, "col"), P("scen", None), P())
    out_specs = P(("col", "scen"), None)
    return jax.shard_map(program, mesh=mesh, in_specs=in_specs, out_specs=out_specs, check_vma=False)
```

```python
import functools

import jax
import jax.numpy as jnp
from jax import lax
from jax.experimental import pallas as pl
from jax.experimental.pallas import tpu as pltpu
from jax.sharding import PartitionSpec as P


BLOCK = 128
SUB = 8


def high(left, right, dims):
    return lax.dot_general(
        left, right, (dims, ((), ())), precision=lax.Precision.HIGH, preferred_element_type=jnp.float32
    )


def full(left, right, dims):
    return lax.dot_general(
        left, right, (dims, ((), ())), precision=lax.Precision.HIGHEST, preferred_element_type=jnp.float32
    )


def eliminate(tiles):
    count, size = len(tiles), tiles[0].shape[1]
    lane = lax.broadcasted_iota(jnp.int32, (SUB, size), 1)
    sub = lax.broadcasted_iota(jnp.int32, (SUB, size), 0)

    def lanes(x, c):
        return jnp.broadcast_to(x[:, c : c + 1], (SUB, size))

    def subs(x, q):
        return jnp.broadcast_to(x[q : q + 1, :], (SUB, size))

    scaled, scales = [], []
    for at in range(count):
        low = SUB * at
        rows = tiles[at]
        cols = [lanes(rows, low + q) for q in range(SUB)]
        inverse, upper, pivots = [], {}, None
        for q in range(SUB):
            pivot = subs(cols[q], q)
            pivots = pivot if pivots is None else jnp.where(sub == q, pivot, pivots)
            inverse.append(1.0 / pivot)
            times = jnp.where(sub > q, cols[q] * inverse[q], 0.0)
            for p in range(q + 1, SUB):
                upper[q, p] = subs(cols[q], p)
                cols[p] = cols[p] - times * upper[q, p]
            pivot_row = jnp.where(lane == low + q, 1.0, subs(rows, q))
            rows = jnp.where((lane == low + q) & (sub > q), 0.0, rows) - times * pivot_row
        pivot_rows = []
        for q in range(SUB):
            row = jnp.where(lane == low + q, 1.0, subs(rows, q))
            pivot_rows.append(jnp.where((lane > low + q) & (lane < low + SUB), 0.0, row))
        own = (lane >= low) & (lane < low + SUB)
        for other in range(at + 1, count):
            tile = tiles[other]
            theirs = [lanes(tile, low + q) for q in range(SUB)]
            tile = jnp.where(own, 0.0, tile)
            times = []
            for q in range(SUB):
                value = theirs[q]
                for p in range(q):
                    value = value - times[p] * upper[p, q]
                value = value * inverse[q]
                times.append(value)
                tile = tile - value * pivot_rows[q]
            tiles[other] = tile
        scale = lax.rsqrt(pivots)
        scales.append(scale)
        scaled.append(rows * scale)
    return scaled, scales


def vmem(count):
    return [pl.BlockSpec(memory_space=pltpu.VMEM)] * count


SMEM = pl.BlockSpec(memory_space=pltpu.SMEM)


def shape(*sizes):
    return jax.ShapeDtypeStruct(sizes, jnp.float32)


def strips(nb):
    for i in range(nb // 2):
        yield i, nb - 1 - i, 0
        yield i, i, (nb - i) * BLOCK


HBM = pl.BlockSpec(memory_space=pltpu.HBM)


def split(x):
    high_part = x.astype(jnp.bfloat16)
    return high_part, (x - high_part.astype(jnp.float32)).astype(jnp.bfloat16)


def three(left, right, dims):
    def one(a, b):
        return lax.dot_general(a, b, (dims, ((), ())), preferred_element_type=jnp.float32)

    (ah, al), (bh, bl) = left, right
    return one(ah, bh) + (one(ah, bl) + one(al, bh))


def product_kernel(edges, tall, place_ref, mask_ref, inverse_hbm, coupling_hbm, *refs):
    count = len(edges) - 1
    pieces = refs[:count]
    keep_a, keep_b, send, panel, rows, ph, plo, qh, ql, rect, sems = refs[count:]
    depth, width = panel.shape
    nb, steps, tile = width // BLOCK, depth // tall, depth // mask_ref.shape[1]
    copies = [pltpu.make_async_copy(coupling_hbm.at[:, pl.ds(0, width)], panel, sems.at[0])]
    for i in range(steps):
        copies.append(pltpu.make_async_copy(inverse_hbm.at[pl.ds(i * tall, tall)], rows.at[i], sems.at[1 + i]))
    for copy in copies:
        copy.start()
    kept = [mask_ref[0, t].astype(jnp.float32) for t in range(depth // tile)]
    copies[0].wait()
    for t in range(depth // tile):
        here = slice(t * tile, (t + 1) * tile)
        ph[here, :], plo[here, :] = split(panel[here, :] * kept[t])
    for i in range(steps):
        copies[1 + i].wait()
        value = three(split(rows[i]), (ph[...], plo[...]), ((1,), (0,)))
        for t in range(i * tall // tile, (i + 1) * tall // tile):
            part = value[t * tile - i * tall : (t + 1) * tile - i * tall, :] * kept[t]
            here = slice(t * tile, (t + 1) * tile)
            qh[here, :], ql[here, :] = split(part)
            for k in range(count):
                lo, hi = max(edges[k], t * tile), min(edges[k + 1], (t + 1) * tile)
                if lo < hi:
                    pieces[k][lo - edges[k] : hi - edges[k], :] = part[lo - t * tile : hi - t * tile, :]
    for i, block, low in strips(nb):
        wide = (block + 1) * BLOCK
        mine = slice(block * BLOCK, wide)
        rect[i * BLOCK : (i + 1) * BLOCK, low : low + wide] = three(
            (ph[:, mine], plo[:, mine]), (qh[:, :wide], ql[:, :wide]), ((0,), (0,))
        )
    half = rect.shape[0] // 2
    core = place_ref[1] & 1
    mine = pl.multiple_of(core * half, half)
    theirs = pl.multiple_of((1 - core) * half, half)
    keep_a[...] = rect[pl.ds(mine, half // 2), :]
    keep_b[...] = rect[pl.ds(mine + half // 2, half // 2), :]
    send[...] = rect[pl.ds(theirs, half), :]


def product(place, mask, inverse, coupling, width, edges):
    depth, count = inverse.shape[0], len(edges) - 1
    nb, tall = width // BLOCK, depth // 4
    high_rows, wide = nb // 2 * BLOCK, (nb + 1) * BLOCK
    return pl.pallas_call(
        functools.partial(product_kernel, edges, tall),
        out_shape=tuple(shape(b - a, width) for a, b in zip(edges, edges[1:]))
        + (shape(high_rows // 4, wide), shape(high_rows // 4, wide), shape(high_rows // 2, wide)),
        in_specs=[SMEM, SMEM, HBM, HBM],
        out_specs=tuple(vmem(count + 3)),
        scratch_shapes=[pltpu.VMEM((depth, width), jnp.float32), pltpu.VMEM((depth // tall, tall, depth), jnp.float32)]
        + [pltpu.VMEM((depth, width), jnp.bfloat16)] * 4
        + [pltpu.VMEM((high_rows, wide), jnp.float32), pltpu.SemaphoreType.DMA((1 + depth // tall,))],
        compiler_params=pltpu.CompilerParams(vmem_limit_bytes=61 << 20),
        cost_estimate=pl.CostEstimate(
            flops=6 * depth * width * (depth + width), bytes_accessed=4 * depth * (depth + 2 * width), transcendentals=0
        ),
    )(place, mask, inverse, coupling)


def collect_kernel(planes, count, place_ref, *refs):
    groups, (out_ref, sems) = refs[: planes * count], refs[planes * count :]
    for h in range(planes):

        @pl.when(place_ref[0] == h)
        def _(h=h):
            low, copies = 0, []
            for k in range(count):
                ref = groups[h * count + k]
                copies.append(pltpu.make_async_copy(ref, out_ref.at[pl.ds(low, ref.shape[0])], sems.at[k]))
                low += ref.shape[0]
            for copy in copies:
                copy.start()
            for copy in copies:
                copy.wait()


def collect(place, groups):
    count = len(groups[0])
    rows, width = sum(x.shape[0] for x in groups[0]), groups[0][0].shape[1]
    return pl.pallas_call(
        functools.partial(collect_kernel, len(groups), count),
        out_shape=shape(rows, width),
        in_specs=[SMEM] + [pl.BlockSpec(memory_space=pl.ANY)] * (len(groups) * count),
        out_specs=vmem(1)[0],
        scratch_shapes=[pltpu.SemaphoreType.DMA((count,))],
        compiler_params=pltpu.CompilerParams(vmem_limit_bytes=8 << 20),
        cost_estimate=pl.CostEstimate(flops=0, bytes_accessed=8 * rows * width, transcendentals=0),
    )(place, *[x for group in groups for x in group])


def part_kernel(place_ref, first_ref, second_ref, keep_ref, send_ref):
    core, wide = place_ref[1] & 1, keep_ref.shape[2]
    for ref, bit in ((keep_ref, core), (send_ref, 1 - core)):
        for j in range(ref.shape[0]):
            here = pl.ds(pl.multiple_of((2 * j + bit) * wide, wide), wide)
            ref[j] = first_ref[:, here] + second_ref[:, here]


def part(place, first, second, scen):
    width, cols = first.shape
    half = shape(scen // 2, width, cols // scen)
    return pl.pallas_call(
        part_kernel,
        out_shape=(half, half),
        in_specs=[SMEM] + vmem(2),
        out_specs=tuple(vmem(2)),
        compiler_params=pltpu.CompilerParams(vmem_limit_bytes=24 << 20),
        cost_estimate=pl.CostEstimate(flops=width * cols, bytes_accessed=12 * width * cols, transcendentals=0),
    )(place, first, second)


def turn_kernel(cuts, place_ref, own_ref, got_ref, *outs):
    for (low, high_row, position, bit), keep_ref, send_ref in zip(cuts, outs[::2], outs[1::2]):
        mine = (place_ref[1] >> bit) & 1
        rows = slice(low, high_row)
        for ref, value in ((keep_ref, mine), (send_ref, 1 - mine)):
            for j in range(ref.shape[0]):
                at = ((j >> position) << (position + 1)) + (j & ((1 << position) - 1)) + (value << position)
                ref[j] = own_ref[at, rows, :] + got_ref[at, rows, :]


def turn(place, own, got, cuts):
    blocks, _, wide = own.shape
    outs = tuple(shape(blocks // 2, high_row - low, wide) for low, high_row, _, _ in cuts for _ in range(2))
    return pl.pallas_call(
        functools.partial(turn_kernel, cuts),
        out_shape=outs,
        in_specs=[SMEM] + vmem(2),
        out_specs=tuple(vmem(len(outs))),
        compiler_params=pltpu.CompilerParams(vmem_limit_bytes=12 << 20),
        cost_estimate=pl.CostEstimate(flops=own.size, bytes_accessed=12 * own.size, transcendentals=0),
    )(place, own, got)


def factor_kernel(place_ref, own_a, own_b, other_a, other_b, diag_ref, own_ref, piece_ref, l_ref, w_ref, rect_ref, base_ref, scale_ref):
    size = w_ref.shape[0]
    nb = size // BLOCK
    plane, me = place_ref[0], place_ref[1]

    @pl.when(plane == 0)
    def _():
        half = rect_ref.shape[0] // 2
        quarter = half // 2
        core = me & 1
        mine = pl.multiple_of(core * half, half)
        theirs = pl.multiple_of((1 - core) * half, half)
        rect_ref[pl.ds(mine, quarter), :] = own_a[...]
        rect_ref[pl.ds(mine + quarter, quarter), :] = own_b[...]
        rect_ref[pl.ds(theirs, quarter), :] = other_a[...]
        rect_ref[pl.ds(theirs + quarter, quarter), :] = other_b[...]
        row = lax.broadcasted_iota(jnp.int32, (BLOCK, BLOCK), 0)
        col = lax.broadcasted_iota(jnp.int32, (BLOCK, BLOCK), 1)
        for i, block, low in strips(nb):
            here = slice(block * BLOCK, (block + 1) * BLOCK)
            for k in range(block + 1):
                there = slice(k * BLOCK, (k + 1) * BLOCK)
                part = rect_ref[i * BLOCK : (i + 1) * BLOCK, low + k * BLOCK : low + (k + 1) * BLOCK]
                if k == block:
                    part = jnp.where(col <= row, part, part.T)
                    part = part + jnp.where(col == row, diag_ref[:, here], 0.0)
                else:
                    w_ref[there, here] = part.T
                w_ref[here, there] = part

        def step(j, carry):
            low = pl.multiple_of(j * BLOCK, BLOCK)
            mine = pl.ds(low, BLOCK)
            tiles = [w_ref[pl.ds(low + SUB * t, SUB), mine] for t in range(BLOCK // SUB)]
            scaled, scales = eliminate(tiles)
            for t in range(BLOCK // SUB):
                base_ref[SUB * t : SUB * t + SUB, :] = scaled[t]
                scale_ref[SUB * t : SUB * t + SUB, :] = scales[t]
            both = base_ref[...]
            inverse = jnp.where(col < row, both, jnp.where(col == row, scale_ref[...], 0.0))
            factor_t = jnp.where(col >= row, both, 0.0)
            below = lax.broadcasted_iota(jnp.int32, (size, BLOCK), 0) >= low + BLOCK
            panel = jnp.where(below, full(w_ref[:, mine], inverse, ((1,), (1,))), 0.0)
            w_ref[mine, :] = full(inverse, w_ref[mine, :], ((1,), (0,)))
            w_ref[mine, mine] = inverse
            pivot_rows = w_ref[mine, :]
            w_ref[:, mine] = jnp.where(below, 0.0, w_ref[:, mine])
            w_ref[...] = w_ref[...] - full(panel, pivot_rows, ((1,), (0,)))
            l_ref[:, mine] = panel
            l_ref[mine, mine] = factor_t.T
            return carry

        lax.fori_loop(0, nb, step, 0)
        for i, block, low in strips(nb):
            for k in range(block + 1):
                rect_ref[i * BLOCK : (i + 1) * BLOCK, low + k * BLOCK : low + (k + 1) * BLOCK] = w_ref[
                    block * BLOCK : (block + 1) * BLOCK, k * BLOCK : (k + 1) * BLOCK
                ]
        rows = own_ref.shape[0]
        first = jnp.minimum(place_ref[2], size - rows)
        own_ref[...] = l_ref[pl.ds(pl.multiple_of(first, rows), rows), :]
        each = piece_ref.shape[0]
        piece_ref[...] = rect_ref[pl.ds(pl.multiple_of(me * each, each), each), :]


def factor(place, parts, diag, each, rows):
    size = diag.shape[1]
    nb = size // BLOCK
    tall, wide = nb // 2 * BLOCK, (nb + 1) * BLOCK
    return pl.pallas_call(
        factor_kernel,
        out_shape=(shape(rows, size), shape(each, wide)),
        in_specs=[SMEM] + vmem(5),
        out_specs=tuple(vmem(2)),
        scratch_shapes=[
            pltpu.VMEM((size, size), jnp.float32),
            pltpu.VMEM((size, size), jnp.float32),
            pltpu.VMEM((tall, wide), jnp.float32),
            pltpu.VMEM((BLOCK, BLOCK), jnp.float32),
            pltpu.VMEM((BLOCK, BLOCK), jnp.float32),
        ],
        compiler_params=pltpu.CompilerParams(vmem_limit_bytes=16 << 20),
        cost_estimate=pl.CostEstimate(flops=20 * size**3, bytes_accessed=12 * size * size, transcendentals=size),
    )(place, *parts, diag)


def last_kernel(count, place_ref, *refs):
    pieces, (keep_a, got_a, keep_b, got_b, own_ref, out_ref, rect_ref, rows_ref) = refs[:count], refs[count:]
    me, first = place_ref[1], place_ref[2]
    rows, width = out_ref.shape
    nb = width // BLOCK
    each = pieces[0].shape[0]
    if len(keep_a.shape) == 3:
        half = keep_a.shape[1]
        rows_ref[:, :half] = (keep_a[0] + got_a[0]).T
        rows_ref[:, half:] = (keep_b[0] + got_b[0]).T
    else:
        half = rows // 2
        rows_ref[:half, :] = keep_a[...] + got_a[...]
        rows_ref[half:, :] = keep_b[...] + got_b[...]
    for m in range(count):
        rect_ref[pl.ds(pl.multiple_of((me ^ m) * each, each), each), :] = pieces[m][...]
    for i, block, low in strips(nb):
        wide = (block + 1) * BLOCK
        part = rect_ref[i * BLOCK : (i + 1) * BLOCK, low : low + wide]
        part = jnp.concatenate(
            [part[:, : wide - BLOCK], jnp.where(
                lax.broadcasted_iota(jnp.int32, (BLOCK, BLOCK), 1) <= lax.broadcasted_iota(jnp.int32, (BLOCK, BLOCK), 0),
                part[:, wide - BLOCK :], 0.0)], axis=1) if wide > BLOCK else part
        out_ref[:, block * BLOCK : (block + 1) * BLOCK] = full(rows_ref[:, :wide], part, ((1,), (1,)))

    @pl.when(first < width)
    def _():
        out_ref[...] = own_ref[...]


def last(place, pieces, sums, own):
    rows, width = own.shape
    nb = width // BLOCK
    tall, wide = nb // 2 * BLOCK, (nb + 1) * BLOCK
    return pl.pallas_call(
        functools.partial(last_kernel, len(pieces)),
        out_shape=shape(rows, width),
        in_specs=[SMEM] + vmem(len(pieces) + 5),
        out_specs=vmem(1)[0],
        scratch_shapes=[pltpu.VMEM((tall, wide), jnp.float32), pltpu.VMEM((rows, width), jnp.float32)],
        compiler_params=pltpu.CompilerParams(vmem_limit_bytes=12 << 20),
        cost_estimate=pl.CostEstimate(flops=6 * rows * width * width, bytes_accessed=8 * width * width, transcendentals=0),
    )(place, *pieces, *sums, own)


def hop(x, source, target):
    return lax.ppermute(x, "col", [(source, target)])


def exchange(x, mask, count):
    return lax.ppermute(x, "scen", [(i, i ^ mask) for i in range(count)])


def orders(count):
    bits = count.bit_length() - 1
    split = 1 + bits // 2
    return bits, list(range(1, split)), list(range(split, bits))


def halve(x, names, bit, count):
    axis = names.index(bit)
    mine = (lax.axis_index("scen") >> bit) & 1
    keep = lax.dynamic_index_in_dim(x, mine, axis, keepdims=False)
    send = lax.dynamic_index_in_dim(x, 1 - mine, axis, keepdims=False)
    return keep, exchange(send, 1 << bit, count), [n for n in names if n != bit]


def scatter_sum(x):
    count = lax.axis_size("scen")
    bits, first, second = orders(count)
    rows = x.shape[0] // count
    x = x.reshape((2,) * bits + (rows,) + x.shape[1:])
    keep, got, names = halve(x, list(range(bits - 1, -1, -1)), 0, count)
    x = keep + got
    lead = (slice(None),) * len(names)
    parts = [x[lead + (slice(0, rows // 2),)], x[lead + (slice(rows // 2, rows),)]]
    lists, pairs = [names, names], [None, None]
    for a, b in zip(first + second, second + first):
        for i, bit in ((0, a), (1, b)):
            if pairs[i] is not None:
                parts[i] = pairs[i][0] + pairs[i][1]
            keep, got, lists[i] = halve(parts[i], lists[i], bit, count)
            pairs[i] = (keep, got)
    return pairs[0] + pairs[1]


def scatter_sum_columns(place, first, second):
    count = lax.axis_size("scen")
    bits, near, far = orders(count)
    half = first.shape[0] // 2
    keep, send = part(place, first, second, count)
    got = exchange(send, 1, count)
    left = [list(range(1, bits)), list(range(1, bits))]
    pairs = None
    for a, b in zip(near + far, far + near):
        if pairs is None:
            cuts = tuple((i * half, (i + 1) * half, left[i].index(bit), bit) for i, bit in ((0, a), (1, b)))
            outs = turn(place, keep, got, cuts)
        else:
            outs = ()
            for i, bit in ((0, a), (1, b)):
                outs += turn(place, *pairs[i], ((0, half, left[i].index(bit), bit),))
        pairs = []
        for i, bit in ((0, a), (1, b)):
            left[i].remove(bit)
            pairs.append((outs[2 * i], exchange(outs[2 * i + 1], 1 << bit, count)))
    return pairs[0] + pairs[1]


PIECES = 8
LATE = 2


def bounds(depth):
    units = depth // SUB
    return [units * k // PIECES * SUB for k in range(PIECES + 1)]


def program(inverses, coupling, tile_mask, hess_diag):
    local = coupling[0]
    width = hess_diag.shape[0]
    scen, planes = lax.axis_size("scen"), lax.axis_size("col")
    me, plane = lax.axis_index("scen").astype(jnp.int32), lax.axis_index("col").astype(jnp.int32)
    rows = local.shape[1] // scen
    place = jnp.stack([plane, me, plane * local.shape[1] + me * rows])
    edge = bounds(local.shape[0])

    *own, keep_a, keep_b, send = product(place, tile_mask, inverses[0], local, width, edge)

    groups = [own]
    for h in range(planes - 1):
        groups.append([hop(groups[h][k], h, h + 1) for k in range(PIECES)])

    got = exchange(send, 1, scen)
    a, b = keep_a + got[: got.shape[0] // 2], keep_b + got[got.shape[0] // 2 :]
    _, near, far = orders(scen)
    for p, q in zip(near + far, far + near):
        got_a = exchange(a, 1 << p, scen)
        got_b = exchange(b, 1 << q, scen)
        a, b = a + got_a, b + got_b
    parts = (a, b, exchange(a, 1, scen), exchange(b, 1, scen))
    each = width // BLOCK // 2 * BLOCK // scen
    lower, piece = factor(place, parts, hess_diag[None, :], each, rows)

    mine = jnp.where(plane == 0, piece, 0.0)
    for h in range(1, planes):
        mine = mine + hop(piece, 0, h)
    pieces = [mine if m == 0 else exchange(mine, m, scen) for m in range(0, scen, 2)]
    pieces = [p for m in range(0, scen, 2) for p in (pieces[m // 2], exchange(pieces[m // 2], 1, scen))]

    cut = PIECES - LATE
    early = edge[cut]
    top = collect(place, [group[:cut] for group in groups])
    bottom = collect(place, [group[cut:] for group in groups])
    if rows % BLOCK == 0:
        first, second = high(top, local[:early], ((0,), (0,))), high(bottom, local[early:], ((0,), (0,)))
        sums = scatter_sum_columns(place, first, second)
    else:
        first, second = high(local[:early], top, ((0,), (0,))), high(local[early:], bottom, ((0,), (0,)))
        sums = scatter_sum(first + second)
    return last(place, pieces, sums, lower)


def solution(mesh):
    in_specs = (P("scen", None, None), P("scen", None, "col"), P("scen", None), P())
    out_specs = P(("col", "scen"), None)
    return jax.shard_map(program, mesh=mesh, in_specs=in_specs, out_specs=out_specs, check_vma=False)
```

```python
import functools

import jax
import jax.numpy as jnp
from jax import lax
from jax.experimental import pallas as pl
from jax.experimental.pallas import tpu as pltpu
from jax.sharding import PartitionSpec as P


BLOCK = 128
SUB = 8


def high(left, right, dims):
    return lax.dot_general(
        left, right, (dims, ((), ())), precision=lax.Precision.HIGH, preferred_element_type=jnp.float32
    )


def full(left, right, dims):
    return lax.dot_general(
        left, right, (dims, ((), ())), precision=lax.Precision.HIGHEST, preferred_element_type=jnp.float32
    )


def eliminate(tiles):
    count, size = len(tiles), tiles[0].shape[1]
    lane = lax.broadcasted_iota(jnp.int32, (SUB, size), 1)
    sub = lax.broadcasted_iota(jnp.int32, (SUB, size), 0)

    def lanes(x, c):
        return jnp.broadcast_to(x[:, c : c + 1], (SUB, size))

    def subs(x, q):
        return jnp.broadcast_to(x[q : q + 1, :], (SUB, size))

    scaled, scales = [], []
    for at in range(count):
        low = SUB * at
        rows = tiles[at]
        cols = [lanes(rows, low + q) for q in range(SUB)]
        inverse, upper, pivots = [], {}, None
        for q in range(SUB):
            pivot = subs(cols[q], q)
            pivots = pivot if pivots is None else jnp.where(sub == q, pivot, pivots)
            inverse.append(1.0 / pivot)
            times = jnp.where(sub > q, cols[q] * inverse[q], 0.0)
            for p in range(q + 1, SUB):
                upper[q, p] = subs(cols[q], p)
                cols[p] = cols[p] - times * upper[q, p]
            pivot_row = jnp.where(lane == low + q, 1.0, subs(rows, q))
            rows = jnp.where((lane == low + q) & (sub > q), 0.0, rows) - times * pivot_row
        pivot_rows = []
        for q in range(SUB):
            row = jnp.where(lane == low + q, 1.0, subs(rows, q))
            pivot_rows.append(jnp.where((lane > low + q) & (lane < low + SUB), 0.0, row))
        own = (lane >= low) & (lane < low + SUB)
        for other in range(at + 1, count):
            tile = tiles[other]
            theirs = [lanes(tile, low + q) for q in range(SUB)]
            tile = jnp.where(own, 0.0, tile)
            times = []
            for q in range(SUB):
                value = theirs[q]
                for p in range(q):
                    value = value - times[p] * upper[p, q]
                value = value * inverse[q]
                times.append(value)
                tile = tile - value * pivot_rows[q]
            tiles[other] = tile
        scale = lax.rsqrt(pivots)
        scales.append(scale)
        scaled.append(rows * scale)
    return scaled, scales


def vmem(count):
    return [pl.BlockSpec(memory_space=pltpu.VMEM)] * count


SMEM = pl.BlockSpec(memory_space=pltpu.SMEM)


def shape(*sizes):
    return jax.ShapeDtypeStruct(sizes, jnp.float32)


def strips(nb):
    for i in range(nb // 2):
        yield i, nb - 1 - i, 0
        yield i, i, (nb - i) * BLOCK


HBM = pl.BlockSpec(memory_space=pltpu.HBM)


def split(x):
    high_part = x.astype(jnp.bfloat16)
    return high_part, (x - high_part.astype(jnp.float32)).astype(jnp.bfloat16)


def three(left, right, dims):
    def one(a, b):
        return lax.dot_general(a, b, (dims, ((), ())), preferred_element_type=jnp.float32)

    (ah, al), (bh, bl) = left, right
    return one(ah, bh) + (one(ah, bl) + one(al, bh))


def product_kernel(edges, tall, place_ref, mask_ref, inverse_hbm, coupling_hbm, *refs):
    count = len(edges) - 1
    pieces = refs[:count]
    keep_a, keep_b, send, panel, rows, ph, plo, qh, ql, rect, sems = refs[count:]

    @pl.when(place_ref[0] == 0)
    def _():
        depth, width = panel.shape
        nb, steps, tile = width // BLOCK, depth // tall, depth // mask_ref.shape[1]
        copies = [pltpu.make_async_copy(coupling_hbm.at[:, pl.ds(0, width)], panel, sems.at[0])]
        for i in range(steps):
            copies.append(pltpu.make_async_copy(inverse_hbm.at[pl.ds(i * tall, tall)], rows.at[i], sems.at[1 + i]))
        for copy in copies:
            copy.start()
        kept = [mask_ref[0, t].astype(jnp.float32) for t in range(depth // tile)]
        copies[0].wait()
        for t in range(depth // tile):
            here = slice(t * tile, (t + 1) * tile)
            ph[here, :], plo[here, :] = split(panel[here, :] * kept[t])
        for i in range(steps):
            copies[1 + i].wait()
            value = three(split(rows[i]), (ph[...], plo[...]), ((1,), (0,)))
            for t in range(i * tall // tile, (i + 1) * tall // tile):
                part = value[t * tile - i * tall : (t + 1) * tile - i * tall, :] * kept[t]
                here = slice(t * tile, (t + 1) * tile)
                qh[here, :], ql[here, :] = split(part)
                for k in range(count):
                    lo, hi = max(edges[k], t * tile), min(edges[k + 1], (t + 1) * tile)
                    if lo < hi:
                        pieces[k][lo - edges[k] : hi - edges[k], :] = part[lo - t * tile : hi - t * tile, :]
        for i, block, low in strips(nb):
            wide = (block + 1) * BLOCK
            mine = slice(block * BLOCK, wide)
            rect[i * BLOCK : (i + 1) * BLOCK, low : low + wide] = three(
                (ph[:, mine], plo[:, mine]), (qh[:, :wide], ql[:, :wide]), ((0,), (0,))
            )
        half = rect.shape[0] // 2
        core = place_ref[1] & 1
        mine = pl.multiple_of(core * half, half)
        theirs = pl.multiple_of((1 - core) * half, half)
        keep_a[...] = rect[pl.ds(mine, half // 2), :]
        keep_b[...] = rect[pl.ds(mine + half // 2, half // 2), :]
        send[...] = rect[pl.ds(theirs, half), :]


def product(place, mask, inverse, coupling, width, edges):
    depth, count = inverse.shape[0], len(edges) - 1
    nb, tall = width // BLOCK, depth // 4
    high_rows, wide = nb // 2 * BLOCK, (nb + 1) * BLOCK
    return pl.pallas_call(
        functools.partial(product_kernel, edges, tall),
        out_shape=tuple(shape(b - a, width) for a, b in zip(edges, edges[1:]))
        + (shape(high_rows // 4, wide), shape(high_rows // 4, wide), shape(high_rows // 2, wide)),
        in_specs=[SMEM, SMEM, HBM, HBM],
        out_specs=tuple(vmem(count + 3)),
        scratch_shapes=[pltpu.VMEM((depth, width), jnp.float32), pltpu.VMEM((depth // tall, tall, depth), jnp.float32)]
        + [pltpu.VMEM((depth, width), jnp.bfloat16)] * 4
        + [pltpu.VMEM((high_rows, wide), jnp.float32), pltpu.SemaphoreType.DMA((1 + depth // tall,))],
        compiler_params=pltpu.CompilerParams(vmem_limit_bytes=61 << 20),
        cost_estimate=pl.CostEstimate(
            flops=6 * depth * width * (depth + width), bytes_accessed=4 * depth * (depth + 2 * width), transcendentals=0
        ),
    )(place, mask, inverse, coupling)


def collect_kernel(planes, count, place_ref, *refs):
    groups, (out_ref, sems) = refs[: planes * count], refs[planes * count :]
    for h in range(planes):

        @pl.when(place_ref[0] == h)
        def _(h=h):
            low, copies = 0, []
            for k in range(count):
                ref = groups[h * count + k]
                copies.append(pltpu.make_async_copy(ref, out_ref.at[pl.ds(low, ref.shape[0])], sems.at[k]))
                low += ref.shape[0]
            for copy in copies:
                copy.start()
            for copy in copies:
                copy.wait()


def collect(place, groups):
    count = len(groups[0])
    rows, width = sum(x.shape[0] for x in groups[0]), groups[0][0].shape[1]
    return pl.pallas_call(
        functools.partial(collect_kernel, len(groups), count),
        out_shape=shape(rows, width),
        in_specs=[SMEM] + [pl.BlockSpec(memory_space=pl.ANY)] * (len(groups) * count),
        out_specs=vmem(1)[0],
        scratch_shapes=[pltpu.SemaphoreType.DMA((count,))],
        compiler_params=pltpu.CompilerParams(vmem_limit_bytes=8 << 20),
        cost_estimate=pl.CostEstimate(flops=0, bytes_accessed=8 * rows * width, transcendentals=0),
    )(place, *[x for group in groups for x in group])


def part_kernel(place_ref, first_ref, second_ref, keep_ref, send_ref):
    core, wide = place_ref[1] & 1, keep_ref.shape[2]
    for ref, bit in ((keep_ref, core), (send_ref, 1 - core)):
        for j in range(ref.shape[0]):
            here = pl.ds(pl.multiple_of((2 * j + bit) * wide, wide), wide)
            ref[j] = first_ref[:, here] + second_ref[:, here]


def part(place, first, second, scen):
    width, cols = first.shape
    half = shape(scen // 2, width, cols // scen)
    return pl.pallas_call(
        part_kernel,
        out_shape=(half, half),
        in_specs=[SMEM] + vmem(2),
        out_specs=tuple(vmem(2)),
        compiler_params=pltpu.CompilerParams(vmem_limit_bytes=24 << 20),
        cost_estimate=pl.CostEstimate(flops=width * cols, bytes_accessed=12 * width * cols, transcendentals=0),
    )(place, first, second)


def turn_kernel(cuts, place_ref, own_ref, got_ref, *outs):
    for (low, high_row, position, bit), keep_ref, send_ref in zip(cuts, outs[::2], outs[1::2]):
        mine = (place_ref[1] >> bit) & 1
        rows = slice(low, high_row)
        for ref, value in ((keep_ref, mine), (send_ref, 1 - mine)):
            for j in range(ref.shape[0]):
                at = ((j >> position) << (position + 1)) + (j & ((1 << position) - 1)) + (value << position)
                ref[j] = own_ref[at, rows, :] + got_ref[at, rows, :]


def turn(place, own, got, cuts):
    blocks, _, wide = own.shape
    outs = tuple(shape(blocks // 2, high_row - low, wide) for low, high_row, _, _ in cuts for _ in range(2))
    return pl.pallas_call(
        functools.partial(turn_kernel, cuts),
        out_shape=outs,
        in_specs=[SMEM] + vmem(2),
        out_specs=tuple(vmem(len(outs))),
        compiler_params=pltpu.CompilerParams(vmem_limit_bytes=12 << 20),
        cost_estimate=pl.CostEstimate(flops=own.size, bytes_accessed=12 * own.size, transcendentals=0),
    )(place, own, got)


def factor_kernel(place_ref, own_a, own_b, other_a, other_b, diag_ref, own_ref, piece_ref, l_ref, w_ref, rect_ref, base_ref, scale_ref):
    size = w_ref.shape[0]
    nb = size // BLOCK
    plane, me = place_ref[0], place_ref[1]

    @pl.when(plane == 0)
    def _():
        half = rect_ref.shape[0] // 2
        quarter = half // 2
        core = me & 1
        mine = pl.multiple_of(core * half, half)
        theirs = pl.multiple_of((1 - core) * half, half)
        rect_ref[pl.ds(mine, quarter), :] = own_a[...]
        rect_ref[pl.ds(mine + quarter, quarter), :] = own_b[...]
        rect_ref[pl.ds(theirs, quarter), :] = other_a[...]
        rect_ref[pl.ds(theirs + quarter, quarter), :] = other_b[...]
        row = lax.broadcasted_iota(jnp.int32, (BLOCK, BLOCK), 0)
        col = lax.broadcasted_iota(jnp.int32, (BLOCK, BLOCK), 1)
        for i, block, low in strips(nb):
            here = slice(block * BLOCK, (block + 1) * BLOCK)
            for k in range(block + 1):
                there = slice(k * BLOCK, (k + 1) * BLOCK)
                part = rect_ref[i * BLOCK : (i + 1) * BLOCK, low + k * BLOCK : low + (k + 1) * BLOCK]
                if k == block:
                    part = jnp.where(col <= row, part, part.T)
                    part = part + jnp.where(col == row, diag_ref[:, here], 0.0)
                w_ref[here, there] = part

        def nt(left, right):
            return full(left, right, ((1,), (1,)))

        def nn(left, right):
            return full(left, right, ((1,), (0,)))

        for j in range(nb):
            low, top = j * BLOCK, (j + 1) * BLOCK
            mine = slice(low, top)
            scaled, scales = eliminate([w_ref[low + SUB * t : low + SUB * (t + 1), mine] for t in range(BLOCK // SUB)])
            for t in range(BLOCK // SUB):
                base_ref[SUB * t : SUB * t + SUB, :] = scaled[t]
                scale_ref[SUB * t : SUB * t + SUB, :] = scales[t]
            both = base_ref[...]
            inverse = jnp.where(col < row, both, jnp.where(col == row, scale_ref[...], 0.0))
            l_ref[mine, mine] = jnp.where(col >= row, both, 0.0).T
            if top < size:
                l_ref[mine, top:] = jnp.zeros((BLOCK, size - top), jnp.float32)
            if j:
                w_ref[mine, :low] = nn(inverse, w_ref[mine, :low])
            w_ref[mine, mine] = inverse
            if top < size:
                panel = nt(w_ref[top:, mine], inverse)
                l_ref[top:, mine] = panel
                for k in range(j + 1, nb):
                    here, skip = slice(k * BLOCK, (k + 1) * BLOCK), (k - j - 1) * BLOCK
                    w_ref[k * BLOCK :, here] = w_ref[k * BLOCK :, here] - nt(panel[skip:], panel[skip : skip + BLOCK])
                if j:
                    w_ref[top:, :low] = w_ref[top:, :low] - nn(panel, w_ref[mine, :low])
                w_ref[top:, mine] = -nn(panel, inverse)
        for i, block, low in strips(nb):
            for k in range(block + 1):
                rect_ref[i * BLOCK : (i + 1) * BLOCK, low + k * BLOCK : low + (k + 1) * BLOCK] = w_ref[
                    block * BLOCK : (block + 1) * BLOCK, k * BLOCK : (k + 1) * BLOCK
                ]
        rows = own_ref.shape[0]
        first = jnp.minimum(place_ref[2], size - rows)
        own_ref[...] = l_ref[pl.ds(pl.multiple_of(first, rows), rows), :]
        each = piece_ref.shape[0]
        piece_ref[...] = rect_ref[pl.ds(pl.multiple_of((me >> 1) * each, each), each), :]


def factor(place, parts, diag, each, rows):
    size = diag.shape[1]
    nb = size // BLOCK
    tall, wide = nb // 2 * BLOCK, (nb + 1) * BLOCK
    return pl.pallas_call(
        factor_kernel,
        out_shape=(shape(rows, size), shape(each, wide)),
        in_specs=[SMEM] + vmem(5),
        out_specs=tuple(vmem(2)),
        scratch_shapes=[
            pltpu.VMEM((size, size), jnp.float32),
            pltpu.VMEM((size, size), jnp.float32),
            pltpu.VMEM((tall, wide), jnp.float32),
            pltpu.VMEM((BLOCK, BLOCK), jnp.float32),
            pltpu.VMEM((BLOCK, BLOCK), jnp.float32),
        ],
        compiler_params=pltpu.CompilerParams(vmem_limit_bytes=16 << 20),
        cost_estimate=pl.CostEstimate(flops=20 * size**3, bytes_accessed=12 * size * size, transcendentals=size),
    )(place, *parts, diag)


def last_kernel(count, place_ref, *refs):
    pieces, (keep_a, got_a, keep_b, got_b, own_ref, out_ref, rect_ref, rows_ref) = refs[:count], refs[count:]
    me, first = place_ref[1], place_ref[2]
    rows, width = out_ref.shape
    nb = width // BLOCK
    each = pieces[0].shape[0]
    if len(keep_a.shape) == 3:
        half = keep_a.shape[1]
        rows_ref[:, :half] = (keep_a[0] + got_a[0]).T
        rows_ref[:, half:] = (keep_b[0] + got_b[0]).T
    else:
        half = rows // 2
        rows_ref[:half, :] = keep_a[...] + got_a[...]
        rows_ref[half:, :] = keep_b[...] + got_b[...]
    for m in range(count):
        rect_ref[pl.ds(pl.multiple_of(((me >> 1) ^ m) * each, each), each), :] = pieces[m][...]
    for i, block, low in strips(nb):
        wide = (block + 1) * BLOCK
        part = rect_ref[i * BLOCK : (i + 1) * BLOCK, low : low + wide]
        part = jnp.concatenate(
            [part[:, : wide - BLOCK], jnp.where(
                lax.broadcasted_iota(jnp.int32, (BLOCK, BLOCK), 1) <= lax.broadcasted_iota(jnp.int32, (BLOCK, BLOCK), 0),
                part[:, wide - BLOCK :], 0.0)], axis=1) if wide > BLOCK else part
        out_ref[:, block * BLOCK : (block + 1) * BLOCK] = three(split(rows_ref[:, :wide]), split(part), ((1,), (1,)))

    @pl.when(first < width)
    def _():
        out_ref[...] = own_ref[...]


def last(place, pieces, sums, own):
    rows, width = own.shape
    nb = width // BLOCK
    tall, wide = nb // 2 * BLOCK, (nb + 1) * BLOCK
    return pl.pallas_call(
        functools.partial(last_kernel, len(pieces)),
        out_shape=shape(rows, width),
        in_specs=[SMEM] + vmem(len(pieces) + 5),
        out_specs=vmem(1)[0],
        scratch_shapes=[pltpu.VMEM((tall, wide), jnp.float32), pltpu.VMEM((rows, width), jnp.float32)],
        compiler_params=pltpu.CompilerParams(vmem_limit_bytes=12 << 20),
        cost_estimate=pl.CostEstimate(flops=6 * rows * width * width, bytes_accessed=8 * width * width, transcendentals=0),
    )(place, *pieces, *sums, own)


def hop(x, source, target):
    return lax.ppermute(x, "col", [(source, target)])


def exchange(x, mask, count):
    return lax.ppermute(x, "scen", [(i, i ^ mask) for i in range(count)])


def orders(count):
    bits = count.bit_length() - 1
    split = 1 + bits // 2
    return bits, list(range(1, split)), list(range(split, bits))


def halve(x, names, bit, count):
    axis = names.index(bit)
    mine = (lax.axis_index("scen") >> bit) & 1
    keep = lax.dynamic_index_in_dim(x, mine, axis, keepdims=False)
    send = lax.dynamic_index_in_dim(x, 1 - mine, axis, keepdims=False)
    return keep, exchange(send, 1 << bit, count), [n for n in names if n != bit]


def scatter_sum(x):
    count = lax.axis_size("scen")
    bits, first, second = orders(count)
    rows = x.shape[0] // count
    x = x.reshape((2,) * bits + (rows,) + x.shape[1:])
    keep, got, names = halve(x, list(range(bits - 1, -1, -1)), 0, count)
    x = keep + got
    lead = (slice(None),) * len(names)
    parts = [x[lead + (slice(0, rows // 2),)], x[lead + (slice(rows // 2, rows),)]]
    lists, pairs = [names, names], [None, None]
    for a, b in zip(first + second, second + first):
        for i, bit in ((0, a), (1, b)):
            if pairs[i] is not None:
                parts[i] = pairs[i][0] + pairs[i][1]
            keep, got, lists[i] = halve(parts[i], lists[i], bit, count)
            pairs[i] = (keep, got)
    return pairs[0] + pairs[1]


def scatter_sum_columns(place, first, second):
    count = lax.axis_size("scen")
    bits, near, far = orders(count)
    half = first.shape[0] // 2
    keep, send = part(place, first, second, count)
    got = exchange(send, 1, count)
    left = [list(range(1, bits)), list(range(1, bits))]
    pairs = None
    for a, b in zip(near + far, far + near):
        if pairs is None:
            cuts = tuple((i * half, (i + 1) * half, left[i].index(bit), bit) for i, bit in ((0, a), (1, b)))
            outs = turn(place, keep, got, cuts)
        else:
            outs = ()
            for i, bit in ((0, a), (1, b)):
                outs += turn(place, *pairs[i], ((0, half, left[i].index(bit), bit),))
        pairs = []
        for i, bit in ((0, a), (1, b)):
            left[i].remove(bit)
            pairs.append((outs[2 * i], exchange(outs[2 * i + 1], 1 << bit, count)))
    return pairs[0] + pairs[1]


PIECES = 8
LATE = 2


def bounds(depth):
    units = depth // SUB
    return [units * k // PIECES * SUB for k in range(PIECES + 1)]


def program(inverses, coupling, tile_mask, hess_diag):
    local = coupling[0]
    width = hess_diag.shape[0]
    scen, planes = lax.axis_size("scen"), lax.axis_size("col")
    me, plane = lax.axis_index("scen").astype(jnp.int32), lax.axis_index("col").astype(jnp.int32)
    rows = local.shape[1] // scen
    place = jnp.stack([plane, me, plane * local.shape[1] + me * rows])
    edge = bounds(local.shape[0])

    *own, keep_a, keep_b, send = product(place, tile_mask, inverses[0], local, width, edge)

    groups = [own]
    for h in range(planes - 1):
        groups.append([hop(groups[h][k], h, h + 1) for k in range(PIECES)])

    got = exchange(send, 1, scen)
    a, b = keep_a + got[: got.shape[0] // 2], keep_b + got[got.shape[0] // 2 :]
    _, near, far = orders(scen)
    for p, q in zip(near + far, far + near):
        got_a = exchange(a, 1 << p, scen)
        got_b = exchange(b, 1 << q, scen)
        a, b = a + got_a, b + got_b
    parts = (a, b, exchange(a, 1, scen), exchange(b, 1, scen))
    each = width // BLOCK // 2 * BLOCK // (scen // 2)
    lower, piece = factor(place, parts, hess_diag[None, :], each, rows)

    mine = jnp.where(plane == 0, piece, 0.0)
    for h in range(1, planes):
        mine = mine + hop(piece, 0, h)
    pieces = [mine if m == 0 else exchange(mine, m, scen) for m in range(0, scen, 2)]

    cut = PIECES - LATE
    early = edge[cut]
    top = collect(place, [group[:cut] for group in groups])
    bottom = collect(place, [group[cut:] for group in groups])
    if rows % BLOCK == 0:
        first, second = high(top, local[:early], ((0,), (0,))), high(bottom, local[early:], ((0,), (0,)))
        sums = scatter_sum_columns(place, first, second)
    else:
        first, second = high(local[:early], top, ((0,), (0,))), high(local[early:], bottom, ((0,), (0,)))
        sums = scatter_sum(first + second)
    return last(place, pieces, sums, lower)


def solution(mesh):
    in_specs = (P("scen", None, None), P("scen", None, "col"), P("scen", None), P())
    out_specs = P(("col", "scen"), None)
    return jax.shard_map(program, mesh=mesh, in_specs=in_specs, out_specs=out_specs, check_vma=False)
```

```python
import functools

import jax
import jax.numpy as jnp
from jax import lax
from jax.experimental import pallas as pl
from jax.experimental.pallas import tpu as pltpu
from jax.sharding import PartitionSpec as P


BLOCK = 128
SUB = 8


def high(left, right, dims):
    return lax.dot_general(
        left, right, (dims, ((), ())), precision=lax.Precision.HIGH, preferred_element_type=jnp.float32
    )


def full(left, right, dims):
    return lax.dot_general(
        left, right, (dims, ((), ())), precision=lax.Precision.HIGHEST, preferred_element_type=jnp.float32
    )


def eliminate(tiles):
    count, size = len(tiles), tiles[0].shape[1]
    lane = lax.broadcasted_iota(jnp.int32, (SUB, size), 1)
    sub = lax.broadcasted_iota(jnp.int32, (SUB, size), 0)

    def lanes(x, c):
        return jnp.broadcast_to(x[:, c : c + 1], (SUB, size))

    def subs(x, q):
        return jnp.broadcast_to(x[q : q + 1, :], (SUB, size))

    def row_times(columns, upper, inverse):
        raw, times = [], []
        for q in range(SUB):
            value = columns[q]
            for p in range(q):
                value = value - times[p] * upper[p, q]
            raw.append(value)
            times.append(value * inverse[q])
        return raw, times

    scaled, scales, ready = [], [], None
    for at in range(count):
        low = SUB * at
        rows = tiles[at]
        cols = ready or [lanes(rows, low + q) for q in range(SUB)]
        if at + 1 < count:
            ready = [lanes(tiles[at + 1], low + SUB + q) for q in range(SUB)]
            below = [lanes(tiles[at + 1], low + q) for q in range(SUB)]
        inverse, upper, pivots, factors = [], {}, None, []
        for q in range(SUB):
            pivot = subs(cols[q], q)
            pivots = pivot if pivots is None else jnp.where(sub == q, pivot, pivots)
            inverse.append(1.0 / pivot)
            factors.append(jnp.where(sub > q, cols[q] * inverse[q], 0.0))
            for p in range(q + 1, SUB):
                upper[q, p] = subs(cols[q], p)
                cols[p] = cols[p] - factors[q] * upper[q, p]
        if at + 1 < count:
            raw, next_times = row_times(below, upper, inverse)
            for q in range(SUB):
                for p in range(SUB):
                    ready[q] = ready[q] - next_times[p] * subs(raw[p], q)
        for q in range(SUB):
            pivot_row = jnp.where(lane == low + q, 1.0, subs(rows, q))
            rows = jnp.where((lane == low + q) & (sub > q), 0.0, rows) - factors[q] * pivot_row
        pivot_rows = []
        for q in range(SUB):
            row = jnp.where(lane == low + q, 1.0, subs(rows, q))
            pivot_rows.append(jnp.where((lane > low + q) & (lane < low + SUB), 0.0, row))
        own = (lane >= low) & (lane < low + SUB)
        for other in range(at + 1, count):
            if other == at + 1:
                times = next_times
            else:
                _, times = row_times([lanes(tiles[other], low + q) for q in range(SUB)], upper, inverse)
            tile = jnp.where(own, 0.0, tiles[other])
            for q in range(SUB):
                tile = tile - times[q] * pivot_rows[q]
            tiles[other] = tile
        scale = lax.rsqrt(pivots)
        scales.append(scale)
        scaled.append(rows * scale)
    return scaled, scales


def vmem(count):
    return [pl.BlockSpec(memory_space=pltpu.VMEM)] * count


SMEM = pl.BlockSpec(memory_space=pltpu.SMEM)


def shape(*sizes):
    return jax.ShapeDtypeStruct(sizes, jnp.float32)


def strips(nb):
    for i in range(nb // 2):
        yield i, nb - 1 - i, 0
        yield i, i, (nb - i) * BLOCK


HBM = pl.BlockSpec(memory_space=pltpu.HBM)


def split(x):
    high_part = x.astype(jnp.bfloat16)
    return high_part, (x - high_part.astype(jnp.float32)).astype(jnp.bfloat16)


def three(left, right, dims):
    def one(a, b):
        return lax.dot_general(a, b, (dims, ((), ())), preferred_element_type=jnp.float32)

    (ah, al), (bh, bl) = left, right
    return one(ah, bh) + (one(ah, bl) + one(al, bh))


def product_kernel(edges, tall, place_ref, mask_ref, inverse_hbm, coupling_hbm, *refs):
    count = len(edges) - 1
    pieces = refs[:count]
    keep_a, keep_b, send, panel, rows, ph, plo, qh, ql, rect, sems = refs[count:]

    @pl.when(place_ref[0] == 0)
    def _():
        depth, width = panel.shape
        nb, steps, tile = width // BLOCK, depth // tall, depth // mask_ref.shape[1]
        copies = [pltpu.make_async_copy(coupling_hbm.at[:, pl.ds(0, width)], panel, sems.at[0])]
        for i in range(steps):
            copies.append(pltpu.make_async_copy(inverse_hbm.at[pl.ds(i * tall, tall)], rows.at[i], sems.at[1 + i]))
        for copy in copies:
            copy.start()
        kept = [mask_ref[0, t].astype(jnp.float32) for t in range(depth // tile)]
        copies[0].wait()
        for t in range(depth // tile):
            here = slice(t * tile, (t + 1) * tile)
            ph[here, :], plo[here, :] = split(panel[here, :] * kept[t])
        for i in range(steps):
            copies[1 + i].wait()
            value = three(split(rows[i]), (ph[...], plo[...]), ((1,), (0,)))
            for t in range(i * tall // tile, (i + 1) * tall // tile):
                part = value[t * tile - i * tall : (t + 1) * tile - i * tall, :] * kept[t]
                here = slice(t * tile, (t + 1) * tile)
                qh[here, :], ql[here, :] = split(part)
                for k in range(count):
                    lo, hi = max(edges[k], t * tile), min(edges[k + 1], (t + 1) * tile)
                    if lo < hi:
                        pieces[k][lo - edges[k] : hi - edges[k], :] = part[lo - t * tile : hi - t * tile, :]
        for i, block, low in strips(nb):
            wide = (block + 1) * BLOCK
            mine = slice(block * BLOCK, wide)
            rect[i * BLOCK : (i + 1) * BLOCK, low : low + wide] = three(
                (ph[:, mine], plo[:, mine]), (qh[:, :wide], ql[:, :wide]), ((0,), (0,))
            )
        half = rect.shape[0] // 2
        core = place_ref[1] & 1
        mine = pl.multiple_of(core * half, half)
        theirs = pl.multiple_of((1 - core) * half, half)
        keep_a[...] = rect[pl.ds(mine, half // 2), :]
        keep_b[...] = rect[pl.ds(mine + half // 2, half // 2), :]
        send[...] = rect[pl.ds(theirs, half), :]


def product(place, mask, inverse, coupling, width, edges):
    depth, count = inverse.shape[0], len(edges) - 1
    nb, tall = width // BLOCK, depth // 4
    high_rows, wide = nb // 2 * BLOCK, (nb + 1) * BLOCK
    return pl.pallas_call(
        functools.partial(product_kernel, edges, tall),
        out_shape=tuple(shape(b - a, width) for a, b in zip(edges, edges[1:]))
        + (shape(high_rows // 4, wide), shape(high_rows // 4, wide), shape(high_rows // 2, wide)),
        in_specs=[SMEM, SMEM, HBM, HBM],
        out_specs=tuple(vmem(count + 3)),
        scratch_shapes=[pltpu.VMEM((depth, width), jnp.float32), pltpu.VMEM((depth // tall, tall, depth), jnp.float32)]
        + [pltpu.VMEM((depth, width), jnp.bfloat16)] * 4
        + [pltpu.VMEM((high_rows, wide), jnp.float32), pltpu.SemaphoreType.DMA((1 + depth // tall,))],
        compiler_params=pltpu.CompilerParams(vmem_limit_bytes=61 << 20),
        cost_estimate=pl.CostEstimate(
            flops=6 * depth * width * (depth + width), bytes_accessed=4 * depth * (depth + 2 * width), transcendentals=0
        ),
    )(place, mask, inverse, coupling)


def collect_kernel(planes, count, place_ref, *refs):
    groups, (out_ref, sems) = refs[: planes * count], refs[planes * count :]
    for h in range(planes):

        @pl.when(place_ref[0] == h)
        def _(h=h):
            low, copies = 0, []
            for k in range(count):
                ref = groups[h * count + k]
                copies.append(pltpu.make_async_copy(ref, out_ref.at[pl.ds(low, ref.shape[0])], sems.at[k]))
                low += ref.shape[0]
            for copy in copies:
                copy.start()
            for copy in copies:
                copy.wait()


def collect(place, groups):
    count = len(groups[0])
    rows, width = sum(x.shape[0] for x in groups[0]), groups[0][0].shape[1]
    return pl.pallas_call(
        functools.partial(collect_kernel, len(groups), count),
        out_shape=shape(rows, width),
        in_specs=[SMEM] + [pl.BlockSpec(memory_space=pl.ANY)] * (len(groups) * count),
        out_specs=vmem(1)[0],
        scratch_shapes=[pltpu.SemaphoreType.DMA((count,))],
        compiler_params=pltpu.CompilerParams(vmem_limit_bytes=8 << 20),
        cost_estimate=pl.CostEstimate(flops=0, bytes_accessed=8 * rows * width, transcendentals=0),
    )(place, *[x for group in groups for x in group])


def part_kernel(place_ref, first_ref, second_ref, keep_ref, send_ref):
    core, wide = place_ref[1] & 1, keep_ref.shape[2]
    for ref, bit in ((keep_ref, core), (send_ref, 1 - core)):
        for j in range(ref.shape[0]):
            here = pl.ds(pl.multiple_of((2 * j + bit) * wide, wide), wide)
            ref[j] = first_ref[:, here] + second_ref[:, here]


def part(place, first, second, scen):
    width, cols = first.shape
    half = shape(scen // 2, width, cols // scen)
    return pl.pallas_call(
        part_kernel,
        out_shape=(half, half),
        in_specs=[SMEM] + vmem(2),
        out_specs=tuple(vmem(2)),
        compiler_params=pltpu.CompilerParams(vmem_limit_bytes=14 << 20),
        cost_estimate=pl.CostEstimate(flops=width * cols, bytes_accessed=12 * width * cols, transcendentals=0),
    )(place, first, second)


def turn_kernel(cuts, place_ref, own_ref, got_ref, *outs):
    for (low, high_row, position, bit), keep_ref, send_ref in zip(cuts, outs[::2], outs[1::2]):
        mine = (place_ref[1] >> bit) & 1
        rows = slice(low, high_row)
        for ref, value in ((keep_ref, mine), (send_ref, 1 - mine)):
            for j in range(ref.shape[0]):
                at = ((j >> position) << (position + 1)) + (j & ((1 << position) - 1)) + (value << position)
                ref[j] = own_ref[at, rows, :] + got_ref[at, rows, :]


def turn(place, own, got, cuts):
    blocks, _, wide = own.shape
    outs = tuple(shape(blocks // 2, high_row - low, wide) for low, high_row, _, _ in cuts for _ in range(2))
    return pl.pallas_call(
        functools.partial(turn_kernel, cuts),
        out_shape=outs,
        in_specs=[SMEM] + vmem(2),
        out_specs=tuple(vmem(len(outs))),
        compiler_params=pltpu.CompilerParams(vmem_limit_bytes=12 << 20),
        cost_estimate=pl.CostEstimate(flops=own.size, bytes_accessed=12 * own.size, transcendentals=0),
    )(place, own, got)


def factor_kernel(place_ref, own_a, own_b, other_a, other_b, diag_ref, own_ref, piece_ref, l_ref, w_ref, rect_ref, base_ref, scale_ref):
    size = w_ref.shape[0]
    nb = size // BLOCK
    plane, me = place_ref[0], place_ref[1]

    @pl.when(plane == 0)
    def _():
        half = rect_ref.shape[0] // 2
        quarter = half // 2
        core = me & 1
        mine = pl.multiple_of(core * half, half)
        theirs = pl.multiple_of((1 - core) * half, half)
        rect_ref[pl.ds(mine, quarter), :] = own_a[...]
        rect_ref[pl.ds(mine + quarter, quarter), :] = own_b[...]
        rect_ref[pl.ds(theirs, quarter), :] = other_a[...]
        rect_ref[pl.ds(theirs + quarter, quarter), :] = other_b[...]
        row = lax.broadcasted_iota(jnp.int32, (BLOCK, BLOCK), 0)
        col = lax.broadcasted_iota(jnp.int32, (BLOCK, BLOCK), 1)
        for i, block, low in strips(nb):
            here = slice(block * BLOCK, (block + 1) * BLOCK)
            for k in range(block + 1):
                there = slice(k * BLOCK, (k + 1) * BLOCK)
                part = rect_ref[i * BLOCK : (i + 1) * BLOCK, low + k * BLOCK : low + (k + 1) * BLOCK]
                if k == block:
                    part = jnp.where(col <= row, part, part.T)
                    part = part + jnp.where(col == row, diag_ref[:, here], 0.0)
                w_ref[here, there] = part

        def nt(left, right):
            return full(left, right, ((1,), (1,)))

        def nn(left, right):
            return full(left, right, ((1,), (0,)))

        for j in range(nb):
            low, top = j * BLOCK, (j + 1) * BLOCK
            mine = slice(low, top)
            scaled, scales = eliminate([w_ref[low + SUB * t : low + SUB * (t + 1), mine] for t in range(BLOCK // SUB)])
            for t in range(BLOCK // SUB):
                base_ref[SUB * t : SUB * t + SUB, :] = scaled[t]
                scale_ref[SUB * t : SUB * t + SUB, :] = scales[t]
            both = base_ref[...]
            inverse = jnp.where(col < row, both, jnp.where(col == row, scale_ref[...], 0.0))
            l_ref[mine, mine] = jnp.where(col >= row, both, 0.0).T
            if top < size:
                l_ref[mine, top:] = jnp.zeros((BLOCK, size - top), jnp.float32)
            if j:
                w_ref[mine, :low] = nn(inverse, w_ref[mine, :low])
            w_ref[mine, mine] = inverse
            if top < size:
                panel = nt(w_ref[top:, mine], inverse)
                l_ref[top:, mine] = panel
                for k in range(j + 1, nb):
                    here, skip = slice(k * BLOCK, (k + 1) * BLOCK), (k - j - 1) * BLOCK
                    w_ref[k * BLOCK :, here] = w_ref[k * BLOCK :, here] - nt(panel[skip:], panel[skip : skip + BLOCK])
                if j:
                    w_ref[top:, :low] = w_ref[top:, :low] - nn(panel, w_ref[mine, :low])
                w_ref[top:, mine] = -nn(panel, inverse)
        for i, block, low in strips(nb):
            for k in range(block + 1):
                rect_ref[i * BLOCK : (i + 1) * BLOCK, low + k * BLOCK : low + (k + 1) * BLOCK] = w_ref[
                    block * BLOCK : (block + 1) * BLOCK, k * BLOCK : (k + 1) * BLOCK
                ]
        rows = own_ref.shape[0]
        first = jnp.minimum(place_ref[2], size - rows)
        own_ref[...] = l_ref[pl.ds(pl.multiple_of(first, rows), rows), :]
        each = piece_ref.shape[0]
        piece_ref[...] = rect_ref[pl.ds(pl.multiple_of(me * each, each), each), :]


def factor(place, parts, diag, each, rows):
    size = diag.shape[1]
    nb = size // BLOCK
    tall, wide = nb // 2 * BLOCK, (nb + 1) * BLOCK
    return pl.pallas_call(
        factor_kernel,
        out_shape=(shape(rows, size), shape(each, wide)),
        in_specs=[SMEM] + vmem(5),
        out_specs=tuple(vmem(2)),
        scratch_shapes=[
            pltpu.VMEM((size, size), jnp.float32),
            pltpu.VMEM((size, size), jnp.float32),
            pltpu.VMEM((tall, wide), jnp.float32),
            pltpu.VMEM((BLOCK, BLOCK), jnp.float32),
            pltpu.VMEM((BLOCK, BLOCK), jnp.float32),
        ],
        compiler_params=pltpu.CompilerParams(vmem_limit_bytes=16 << 20),
        cost_estimate=pl.CostEstimate(flops=20 * size**3, bytes_accessed=12 * size * size, transcendentals=size),
    )(place, *parts, diag)


def last_kernel(count, place_ref, *refs):
    pieces, (keep_a, got_a, keep_b, got_b, own_ref, out_ref, rect_ref, rows_ref) = refs[:count], refs[count:]
    me, first = place_ref[1], place_ref[2]
    rows, width = out_ref.shape
    nb = width // BLOCK
    each = pieces[0].shape[0]
    if len(keep_a.shape) == 3:
        half = keep_a.shape[1]
        rows_ref[:, :half] = (keep_a[0] + got_a[0]).T
        rows_ref[:, half:] = (keep_b[0] + got_b[0]).T
    else:
        half = rows // 2
        rows_ref[:half, :] = keep_a[...] + got_a[...]
        rows_ref[half:, :] = keep_b[...] + got_b[...]
    for m in range(count):
        rect_ref[pl.ds(pl.multiple_of((me ^ m) * each, each), each), :] = pieces[m][...]
    for i, block, low in strips(nb):
        wide = (block + 1) * BLOCK
        part = rect_ref[i * BLOCK : (i + 1) * BLOCK, low : low + wide]
        part = jnp.concatenate(
            [part[:, : wide - BLOCK], jnp.where(
                lax.broadcasted_iota(jnp.int32, (BLOCK, BLOCK), 1) <= lax.broadcasted_iota(jnp.int32, (BLOCK, BLOCK), 0),
                part[:, wide - BLOCK :], 0.0)], axis=1) if wide > BLOCK else part
        out_ref[:, block * BLOCK : (block + 1) * BLOCK] = three(split(rows_ref[:, :wide]), split(part), ((1,), (1,)))

    @pl.when(first < width)
    def _():
        out_ref[...] = own_ref[...]


def last(place, pieces, sums, own):
    rows, width = own.shape
    nb = width // BLOCK
    tall, wide = nb // 2 * BLOCK, (nb + 1) * BLOCK
    return pl.pallas_call(
        functools.partial(last_kernel, len(pieces)),
        out_shape=shape(rows, width),
        in_specs=[SMEM] + vmem(len(pieces) + 5),
        out_specs=vmem(1)[0],
        scratch_shapes=[pltpu.VMEM((tall, wide), jnp.float32), pltpu.VMEM((rows, width), jnp.float32)],
        compiler_params=pltpu.CompilerParams(vmem_limit_bytes=12 << 20),
        cost_estimate=pl.CostEstimate(flops=6 * rows * width * width, bytes_accessed=8 * width * width, transcendentals=0),
    )(place, *pieces, *sums, own)


def hop(x, source, target):
    return lax.ppermute(x, "col", [(source, target)])


def exchange(x, mask, count):
    return lax.ppermute(x, "scen", [(i, i ^ mask) for i in range(count)])


def orders(count):
    bits = count.bit_length() - 1
    split = 1 + bits // 2
    return bits, list(range(1, split)), list(range(split, bits))


def halve(x, names, bit, count):
    axis = names.index(bit)
    mine = (lax.axis_index("scen") >> bit) & 1
    keep = lax.dynamic_index_in_dim(x, mine, axis, keepdims=False)
    send = lax.dynamic_index_in_dim(x, 1 - mine, axis, keepdims=False)
    return keep, exchange(send, 1 << bit, count), [n for n in names if n != bit]


def scatter_sum(x):
    count = lax.axis_size("scen")
    bits, first, second = orders(count)
    rows = x.shape[0] // count
    x = x.reshape((2,) * bits + (rows,) + x.shape[1:])
    keep, got, names = halve(x, list(range(bits - 1, -1, -1)), 0, count)
    x = keep + got
    lead = (slice(None),) * len(names)
    parts = [x[lead + (slice(0, rows // 2),)], x[lead + (slice(rows // 2, rows),)]]
    lists, pairs = [names, names], [None, None]
    for a, b in zip(first + second, second + first):
        for i, bit in ((0, a), (1, b)):
            if pairs[i] is not None:
                parts[i] = pairs[i][0] + pairs[i][1]
            keep, got, lists[i] = halve(parts[i], lists[i], bit, count)
            pairs[i] = (keep, got)
    return pairs[0] + pairs[1]


def scatter_sum_columns(place, first, second):
    count = lax.axis_size("scen")
    bits, near, far = orders(count)
    half = first.shape[0] // 2
    keep, send = part(place, first, second, count)
    got = exchange(send, 1, count)
    left = [list(range(1, bits)), list(range(1, bits))]
    pairs = None
    for a, b in zip(near + far, far + near):
        if pairs is None:
            cuts = tuple((i * half, (i + 1) * half, left[i].index(bit), bit) for i, bit in ((0, a), (1, b)))
            outs = turn(place, keep, got, cuts)
        else:
            outs = ()
            for i, bit in ((0, a), (1, b)):
                outs += turn(place, *pairs[i], ((0, half, left[i].index(bit), bit),))
        pairs = []
        for i, bit in ((0, a), (1, b)):
            left[i].remove(bit)
            pairs.append((outs[2 * i], exchange(outs[2 * i + 1], 1 << bit, count)))
    return pairs[0] + pairs[1]


PIECES = 8
LATE = 1


def bounds(depth):
    units = depth // SUB
    return [units * k // PIECES * SUB for k in range(PIECES + 1)]


def program(inverses, coupling, tile_mask, hess_diag):
    local = coupling[0]
    width = hess_diag.shape[0]
    scen, planes = lax.axis_size("scen"), lax.axis_size("col")
    me, plane = lax.axis_index("scen").astype(jnp.int32), lax.axis_index("col").astype(jnp.int32)
    rows = local.shape[1] // scen
    place = jnp.stack([plane, me, plane * local.shape[1] + me * rows])
    edge = bounds(local.shape[0])

    *own, keep_a, keep_b, send = product(place, tile_mask, inverses[0], local, width, edge)

    groups = [own]
    for h in range(planes - 1):
        groups.append([hop(groups[h][k], h, h + 1) for k in range(PIECES)])

    got = exchange(send, 1, scen)
    a, b = keep_a + got[: got.shape[0] // 2], keep_b + got[got.shape[0] // 2 :]
    _, near, far = orders(scen)
    for p, q in zip(near + far, far + near):
        got_a = exchange(a, 1 << p, scen)
        got_b = exchange(b, 1 << q, scen)
        a, b = a + got_a, b + got_b
    parts = (a, b, exchange(a, 1, scen), exchange(b, 1, scen))
    each = width // BLOCK // 2 * BLOCK // scen
    lower, piece = factor(place, parts, hess_diag[None, :], each, rows)

    mine = jnp.where(plane == 0, piece, 0.0)
    for h in range(1, planes):
        mine = mine + hop(piece, 0, h)
    pieces = [mine if m == 0 else exchange(mine, m, scen) for m in range(0, scen, 2)]
    pieces = [p for m in range(0, scen, 2) for p in (pieces[m // 2], exchange(pieces[m // 2], 1, scen))]

    cut = PIECES - LATE
    early = edge[cut]
    top = collect(place, [group[:cut] for group in groups])
    bottom = collect(place, [group[cut:] for group in groups])
    if rows % BLOCK == 0:
        first, second = high(top, local[:early], ((0,), (0,))), high(bottom, local[early:], ((0,), (0,)))
        sums = scatter_sum_columns(place, first, second)
    else:
        first, second = high(local[:early], top, ((0,), (0,))), high(local[early:], bottom, ((0,), (0,)))
        sums = scatter_sum(first + second)
    return last(place, pieces, sums, lower)


def solution(mesh):
    in_specs = (P("scen", None, None), P("scen", None, "col"), P("scen", None), P())
    out_specs = P(("col", "scen"), None)
    return jax.shard_map(program, mesh=mesh, in_specs=in_specs, out_specs=out_specs, check_vma=False)
```

```python
import functools

import jax
import jax.numpy as jnp
from jax import lax
from jax.experimental import pallas as pl
from jax.experimental.pallas import tpu as pltpu
from jax.sharding import PartitionSpec as P


BLOCK = 128
SUB = 8


def high(left, right, dims):
    return lax.dot_general(
        left, right, (dims, ((), ())), precision=lax.Precision.HIGH, preferred_element_type=jnp.float32
    )


def full(left, right, dims):
    return lax.dot_general(
        left, right, (dims, ((), ())), precision=lax.Precision.HIGHEST, preferred_element_type=jnp.float32
    )


def eliminate(tiles):
    count, size = len(tiles), tiles[0].shape[1]
    lane = lax.broadcasted_iota(jnp.int32, (SUB, size), 1)
    sub = lax.broadcasted_iota(jnp.int32, (SUB, size), 0)

    def lanes(x, c):
        return jnp.broadcast_to(x[:, c : c + 1], (SUB, size))

    def subs(x, q):
        return jnp.broadcast_to(x[q : q + 1, :], (SUB, size))

    def row_times(columns, upper, inverse):
        raw, times = [], []
        for q in range(SUB):
            value = columns[q]
            for p in range(q):
                value = value - times[p] * upper[p, q]
            raw.append(value)
            times.append(value * inverse[q])
        return raw, times

    scaled, scales, ready = [], [], None
    for at in range(count):
        low = SUB * at
        rows = tiles[at]
        cols = ready or [lanes(rows, low + q) for q in range(SUB)]
        if at + 1 < count:
            ready = [lanes(tiles[at + 1], low + SUB + q) for q in range(SUB)]
            below = [lanes(tiles[at + 1], low + q) for q in range(SUB)]
        inverse, upper, pivots, factors = [], {}, None, []
        for q in range(SUB):
            pivot = subs(cols[q], q)
            pivots = pivot if pivots is None else jnp.where(sub == q, pivot, pivots)
            inverse.append(1.0 / pivot)
            factors.append(jnp.where(sub > q, cols[q] * inverse[q], 0.0))
            for p in range(q + 1, SUB):
                upper[q, p] = subs(cols[q], p)
                cols[p] = cols[p] - factors[q] * upper[q, p]
        if at + 1 < count:
            raw, next_times = row_times(below, upper, inverse)
            for q in range(SUB):
                for p in range(SUB):
                    ready[q] = ready[q] - next_times[p] * subs(raw[p], q)
        for q in range(SUB):
            pivot_row = jnp.where(lane == low + q, 1.0, subs(rows, q))
            rows = jnp.where((lane == low + q) & (sub > q), 0.0, rows) - factors[q] * pivot_row
        pivot_rows = []
        for q in range(SUB):
            row = jnp.where(lane == low + q, 1.0, subs(rows, q))
            pivot_rows.append(jnp.where((lane > low + q) & (lane < low + SUB), 0.0, row))
        own = (lane >= low) & (lane < low + SUB)
        for other in range(at + 1, count):
            if other == at + 1:
                times = next_times
            else:
                _, times = row_times([lanes(tiles[other], low + q) for q in range(SUB)], upper, inverse)
            tile = jnp.where(own, 0.0, tiles[other])
            for q in range(SUB):
                tile = tile - times[q] * pivot_rows[q]
            tiles[other] = tile
        scale = lax.rsqrt(pivots)
        scales.append(scale)
        scaled.append(rows * scale)
    return scaled, scales


def vmem(count):
    return [pl.BlockSpec(memory_space=pltpu.VMEM)] * count


SMEM = pl.BlockSpec(memory_space=pltpu.SMEM)


def shape(*sizes):
    return jax.ShapeDtypeStruct(sizes, jnp.float32)


def strips(nb):
    for i in range(nb // 2):
        yield i, nb - 1 - i, 0
        yield i, i, (nb - i) * BLOCK


HBM = pl.BlockSpec(memory_space=pltpu.HBM)


def split(x):
    high_part = x.astype(jnp.bfloat16)
    return high_part, (x - high_part.astype(jnp.float32)).astype(jnp.bfloat16)


def three(left, right, dims):
    def one(a, b):
        return lax.dot_general(a, b, (dims, ((), ())), preferred_element_type=jnp.float32)

    (ah, al), (bh, bl) = left, right
    return one(ah, bh) + (one(ah, bl) + one(al, bh))


def product_kernel(edges, tall, place_ref, mask_ref, inverse_hbm, coupling_hbm, *refs):
    count = len(edges) - 1
    pieces = refs[:count]
    keep, send, panel, rows, ph, plo, qh, ql, rect, sems = refs[count:]

    @pl.when(place_ref[0] == 0)
    def _():
        depth, width = panel.shape
        nb, steps, tile = width // BLOCK, depth // tall, depth // mask_ref.shape[1]
        copies = [pltpu.make_async_copy(coupling_hbm.at[:, pl.ds(0, width)], panel, sems.at[0])]
        for i in range(steps):
            copies.append(pltpu.make_async_copy(inverse_hbm.at[pl.ds(i * tall, tall)], rows.at[i], sems.at[1 + i]))
        for copy in copies:
            copy.start()
        kept = [mask_ref[0, t].astype(jnp.float32) for t in range(depth // tile)]
        copies[0].wait()
        for t in range(depth // tile):
            here = slice(t * tile, (t + 1) * tile)
            ph[here, :], plo[here, :] = split(panel[here, :] * kept[t])
        for i in range(steps):
            copies[1 + i].wait()
            value = three(split(rows[i]), (ph[...], plo[...]), ((1,), (0,)))
            for t in range(i * tall // tile, (i + 1) * tall // tile):
                part = value[t * tile - i * tall : (t + 1) * tile - i * tall, :] * kept[t]
                here = slice(t * tile, (t + 1) * tile)
                qh[here, :], ql[here, :] = split(part)
                for k in range(count):
                    lo, hi = max(edges[k], t * tile), min(edges[k + 1], (t + 1) * tile)
                    if lo < hi:
                        pieces[k][lo - edges[k] : hi - edges[k], :] = part[lo - t * tile : hi - t * tile, :]
        for i, block, low in strips(nb):
            wide = (block + 1) * BLOCK
            mine = slice(block * BLOCK, wide)
            rect[i * BLOCK : (i + 1) * BLOCK, low : low + wide] = three(
                (ph[:, mine], plo[:, mine]), (qh[:, :wide], ql[:, :wide]), ((0,), (0,))
            )
        half = rect.shape[0] // 2
        core = place_ref[1] & 1
        mine = pl.multiple_of(core * half, half)
        theirs = pl.multiple_of((1 - core) * half, half)
        keep[...] = rect[pl.ds(mine, half), :]
        send[...] = rect[pl.ds(theirs, half), :]


def product(place, mask, inverse, coupling, width, edges):
    depth, count = inverse.shape[0], len(edges) - 1
    nb, tall = width // BLOCK, depth // 4
    high_rows, wide = nb // 2 * BLOCK, (nb + 1) * BLOCK
    return pl.pallas_call(
        functools.partial(product_kernel, edges, tall),
        out_shape=tuple(shape(b - a, width) for a, b in zip(edges, edges[1:]))
        + (shape(high_rows // 2, wide), shape(high_rows // 2, wide)),
        in_specs=[SMEM, SMEM, HBM, HBM],
        out_specs=tuple(vmem(count + 2)),
        scratch_shapes=[pltpu.VMEM((depth, width), jnp.float32), pltpu.VMEM((depth // tall, tall, depth), jnp.float32)]
        + [pltpu.VMEM((depth, width), jnp.bfloat16)] * 4
        + [pltpu.VMEM((high_rows, wide), jnp.float32), pltpu.SemaphoreType.DMA((1 + depth // tall,))],
        compiler_params=pltpu.CompilerParams(vmem_limit_bytes=61 << 20),
        cost_estimate=pl.CostEstimate(
            flops=6 * depth * width * (depth + width), bytes_accessed=4 * depth * (depth + 2 * width), transcendentals=0
        ),
    )(place, mask, inverse, coupling)


def collect_kernel(planes, count, place_ref, *refs):
    groups, (out_ref, sems) = refs[: planes * count], refs[planes * count :]
    for h in range(planes):

        @pl.when(place_ref[0] == h)
        def _(h=h):
            low, copies = 0, []
            for k in range(count):
                ref = groups[h * count + k]
                copies.append(pltpu.make_async_copy(ref, out_ref.at[pl.ds(low, ref.shape[0])], sems.at[k]))
                low += ref.shape[0]
            for copy in copies:
                copy.start()
            for copy in copies:
                copy.wait()


def collect(place, groups):
    count = len(groups[0])
    rows, width = sum(x.shape[0] for x in groups[0]), groups[0][0].shape[1]
    return pl.pallas_call(
        functools.partial(collect_kernel, len(groups), count),
        out_shape=shape(rows, width),
        in_specs=[SMEM] + [pl.BlockSpec(memory_space=pl.ANY)] * (len(groups) * count),
        out_specs=vmem(1)[0],
        scratch_shapes=[pltpu.SemaphoreType.DMA((count,))],
        compiler_params=pltpu.CompilerParams(vmem_limit_bytes=8 << 20),
        cost_estimate=pl.CostEstimate(flops=0, bytes_accessed=8 * rows * width, transcendentals=0),
    )(place, *[x for group in groups for x in group])


def part_kernel(place_ref, first_ref, second_ref, keep_ref, send_ref):
    core, wide = place_ref[1] & 1, keep_ref.shape[2]
    for ref, bit in ((keep_ref, core), (send_ref, 1 - core)):
        for j in range(ref.shape[0]):
            here = pl.ds(pl.multiple_of((2 * j + bit) * wide, wide), wide)
            ref[j] = first_ref[:, here] + second_ref[:, here]


def part(place, first, second, scen):
    width, cols = first.shape
    half = shape(scen // 2, width, cols // scen)
    return pl.pallas_call(
        part_kernel,
        out_shape=(half, half),
        in_specs=[SMEM] + vmem(2),
        out_specs=tuple(vmem(2)),
        compiler_params=pltpu.CompilerParams(vmem_limit_bytes=14 << 20),
        cost_estimate=pl.CostEstimate(flops=width * cols, bytes_accessed=12 * width * cols, transcendentals=0),
    )(place, first, second)


def turn_kernel(near, far, place_ref, own_ref, got_ref, keep_ref, send_ref):
    core = place_ref[1] & 1
    bit, position = (jnp.where(core == 0, near[i], far[i]) for i in range(2))
    mine = (place_ref[1] >> bit) & 1
    for ref, value in ((keep_ref, mine), (send_ref, 1 - mine)):
        for j in range(ref.shape[0]):
            at = ((j >> position) << (position + 1)) + (j & ((1 << position) - 1)) + (value << position)
            ref[j] = own_ref[at] + got_ref[at]


def turn(place, own, got, near, far):
    half = shape(own.shape[0] // 2, *own.shape[1:])
    return pl.pallas_call(
        functools.partial(turn_kernel, near, far),
        out_shape=(half, half),
        in_specs=[SMEM] + vmem(2),
        out_specs=tuple(vmem(2)),
        compiler_params=pltpu.CompilerParams(vmem_limit_bytes=12 << 20),
        cost_estimate=pl.CostEstimate(flops=own.size, bytes_accessed=12 * own.size, transcendentals=0),
    )(place, own, got)


def factor_kernel(place_ref, strip, other, diag_ref, own_ref, piece_ref, l_ref, w_ref, rect_ref, base_ref, scale_ref):
    size = w_ref.shape[0]
    nb = size // BLOCK
    plane, me = place_ref[0], place_ref[1]

    @pl.when(plane == 0)
    def _():
        half = rect_ref.shape[0] // 2
        core = me & 1
        mine = pl.multiple_of(core * half, half)
        theirs = pl.multiple_of((1 - core) * half, half)
        rect_ref[pl.ds(mine, half), :] = strip[...]
        rect_ref[pl.ds(theirs, half), :] = other[...]
        row = lax.broadcasted_iota(jnp.int32, (BLOCK, BLOCK), 0)
        col = lax.broadcasted_iota(jnp.int32, (BLOCK, BLOCK), 1)
        for i, block, low in strips(nb):
            here = slice(block * BLOCK, (block + 1) * BLOCK)
            for k in range(block + 1):
                there = slice(k * BLOCK, (k + 1) * BLOCK)
                part = rect_ref[i * BLOCK : (i + 1) * BLOCK, low + k * BLOCK : low + (k + 1) * BLOCK]
                if k == block:
                    part = jnp.where(col <= row, part, part.T)
                    part = part + jnp.where(col == row, diag_ref[:, here], 0.0)
                w_ref[here, there] = part

        def nt(left, right):
            return full(left, right, ((1,), (1,)))

        def nn(left, right):
            return full(left, right, ((1,), (0,)))

        for j in range(nb):
            low, top = j * BLOCK, (j + 1) * BLOCK
            mine = slice(low, top)
            scaled, scales = eliminate([w_ref[low + SUB * t : low + SUB * (t + 1), mine] for t in range(BLOCK // SUB)])
            for t in range(BLOCK // SUB):
                base_ref[SUB * t : SUB * t + SUB, :] = scaled[t]
                scale_ref[SUB * t : SUB * t + SUB, :] = scales[t]
            both = base_ref[...]
            inverse = jnp.where(col < row, both, jnp.where(col == row, scale_ref[...], 0.0))
            l_ref[mine, mine] = jnp.where(col >= row, both, 0.0).T
            if top < size:
                l_ref[mine, top:] = jnp.zeros((BLOCK, size - top), jnp.float32)
            if j:
                w_ref[mine, :low] = nn(inverse, w_ref[mine, :low])
            w_ref[mine, mine] = inverse
            if top < size:
                panel = nt(w_ref[top:, mine], inverse)
                l_ref[top:, mine] = panel
                for k in range(j + 1, nb):
                    here, skip = slice(k * BLOCK, (k + 1) * BLOCK), (k - j - 1) * BLOCK
                    w_ref[k * BLOCK :, here] = w_ref[k * BLOCK :, here] - nt(panel[skip:], panel[skip : skip + BLOCK])
                if j:
                    w_ref[top:, :low] = w_ref[top:, :low] - nn(panel, w_ref[mine, :low])
                w_ref[top:, mine] = -nn(panel, inverse)
        for i, block, low in strips(nb):
            for k in range(block + 1):
                rect_ref[i * BLOCK : (i + 1) * BLOCK, low + k * BLOCK : low + (k + 1) * BLOCK] = w_ref[
                    block * BLOCK : (block + 1) * BLOCK, k * BLOCK : (k + 1) * BLOCK
                ]
        rows = own_ref.shape[0]
        first = jnp.minimum(place_ref[2], size - rows)
        own_ref[...] = l_ref[pl.ds(pl.multiple_of(first, rows), rows), :]
        each = piece_ref.shape[0]
        piece_ref[...] = rect_ref[pl.ds(pl.multiple_of(me * each, each), each), :]


def factor(place, parts, diag, each, rows):
    size = diag.shape[1]
    nb = size // BLOCK
    tall, wide = nb // 2 * BLOCK, (nb + 1) * BLOCK
    return pl.pallas_call(
        factor_kernel,
        out_shape=(shape(rows, size), shape(each, wide)),
        in_specs=[SMEM] + vmem(3),
        out_specs=tuple(vmem(2)),
        scratch_shapes=[
            pltpu.VMEM((size, size), jnp.float32),
            pltpu.VMEM((size, size), jnp.float32),
            pltpu.VMEM((tall, wide), jnp.float32),
            pltpu.VMEM((BLOCK, BLOCK), jnp.float32),
            pltpu.VMEM((BLOCK, BLOCK), jnp.float32),
        ],
        compiler_params=pltpu.CompilerParams(vmem_limit_bytes=16 << 20),
        cost_estimate=pl.CostEstimate(flops=20 * size**3, bytes_accessed=12 * size * size, transcendentals=size),
    )(place, *parts, diag)


def last_kernel(count, place_ref, *refs):
    pieces, (sums, got, own_ref, out_ref, rect_ref, rows_ref) = refs[:count], refs[count:]
    me, first = place_ref[1], place_ref[2]
    _, width = out_ref.shape
    nb = width // BLOCK
    each = pieces[0].shape[0]
    total = sums[...] + got[...]
    rows_ref[...] = total[0].T if len(sums.shape) == 3 else total
    for m in range(count):
        rect_ref[pl.ds(pl.multiple_of((me ^ m) * each, each), each), :] = pieces[m][...]
    for i, block, low in strips(nb):
        wide = (block + 1) * BLOCK
        part = rect_ref[i * BLOCK : (i + 1) * BLOCK, low : low + wide]
        part = jnp.concatenate(
            [part[:, : wide - BLOCK], jnp.where(
                lax.broadcasted_iota(jnp.int32, (BLOCK, BLOCK), 1) <= lax.broadcasted_iota(jnp.int32, (BLOCK, BLOCK), 0),
                part[:, wide - BLOCK :], 0.0)], axis=1) if wide > BLOCK else part
        out_ref[:, block * BLOCK : (block + 1) * BLOCK] = three(split(rows_ref[:, :wide]), split(part), ((1,), (1,)))

    @pl.when(first < width)
    def _():
        out_ref[...] = own_ref[...]


def last(place, pieces, sums, own):
    rows, width = own.shape
    nb = width // BLOCK
    tall, wide = nb // 2 * BLOCK, (nb + 1) * BLOCK
    return pl.pallas_call(
        functools.partial(last_kernel, len(pieces)),
        out_shape=shape(rows, width),
        in_specs=[SMEM] + vmem(len(pieces) + 3),
        out_specs=vmem(1)[0],
        scratch_shapes=[pltpu.VMEM((tall, wide), jnp.float32), pltpu.VMEM((rows, width), jnp.float32)],
        compiler_params=pltpu.CompilerParams(vmem_limit_bytes=12 << 20),
        cost_estimate=pl.CostEstimate(flops=6 * rows * width * width, bytes_accessed=8 * width * width, transcendentals=0),
    )(place, *pieces, *sums, own)


def hop(x, source, target):
    return lax.ppermute(x, "col", [(source, target)])


def exchange(x, mask, count):
    return lax.ppermute(x, "scen", [(i, i ^ mask) for i in range(count)])


def orders(count):
    bits = count.bit_length() - 1
    split = 1 + bits // 2
    first, second = list(range(1, split)), list(range(split, bits))
    return bits, first + second, second + first


def crossed(x, near, far, count):
    return lax.ppermute(x, "scen", [(i, i ^ (1 << (far if i & 1 else near))) for i in range(count)])


def scatter_sum(x):
    count = lax.axis_size("scen")
    bits, near, far = orders(count)
    me = lax.axis_index("scen")
    core = me & 1
    x = x.reshape((count // 2, 2, x.shape[0] // count) + x.shape[1:])
    keep = lax.dynamic_index_in_dim(x, core, 1, keepdims=False)
    got = exchange(lax.dynamic_index_in_dim(x, 1 - core, 1, keepdims=False), 1, count)
    left = [list(range(1, bits)), list(range(1, bits))]
    for a, b in zip(near, far):
        x = keep + got
        tall = x.shape[0] // 2
        picks = []
        for i, bit in ((0, a), (1, b)):
            position = left[i].index(bit)
            left[i].remove(bit)
            mine = (me >> bit) & 1
            j = jnp.arange(tall)
            base = ((j >> position) << (position + 1)) + (j & ((1 << position) - 1))
            picks.append((base + (mine << position), base + ((1 - mine) << position)))
        keep, send = (jnp.take(x, jnp.where(core == 0, picks[0][i], picks[1][i]), axis=0) for i in range(2))
        got = crossed(send, a, b, count)
    return keep[0], got[0]


def scatter_sum_columns(place, first, second):
    count = lax.axis_size("scen")
    bits, near, far = orders(count)
    keep, send = part(place, first, second, count)
    got = exchange(send, 1, count)
    left = [list(range(1, bits)), list(range(1, bits))]
    for a, b in zip(near, far):
        keep, send = turn(place, keep, got, (a, left[0].index(a)), (b, left[1].index(b)))
        left[0].remove(a)
        left[1].remove(b)
        got = crossed(send, a, b, count)
    return keep, got


PIECES = 8
LATE = 1


def bounds(depth):
    units = depth // SUB
    return [units * k // PIECES * SUB for k in range(PIECES + 1)]


def program(inverses, coupling, tile_mask, hess_diag):
    local = coupling[0]
    width = hess_diag.shape[0]
    scen, planes = lax.axis_size("scen"), lax.axis_size("col")
    me, plane = lax.axis_index("scen").astype(jnp.int32), lax.axis_index("col").astype(jnp.int32)
    rows = local.shape[1] // scen
    place = jnp.stack([plane, me, plane * local.shape[1] + me * rows])
    edge = bounds(local.shape[0])

    *own, strip, send = product(place, tile_mask, inverses[0], local, width, edge)

    groups = [own]
    for h in range(planes - 1):
        groups.append([hop(groups[h][k], h, h + 1) for k in range(PIECES)])

    strip = strip + exchange(send, 1, scen)
    _, near, far = orders(scen)
    for p, q in zip(near, far):
        strip = strip + crossed(strip, p, q, scen)
    other = exchange(strip, 1, scen)
    each = width // BLOCK // 2 * BLOCK // scen
    lower, piece = factor(place, (strip, other), hess_diag[None, :], each, rows)

    mine = jnp.where(plane == 0, piece, 0.0)
    for h in range(1, planes):
        piece = hop(piece, h - 1, h)
        mine = mine + piece
    pieces = [mine if m == 0 else exchange(mine, m, scen) for m in range(0, scen, 2)]
    pieces = [p for m in range(0, scen, 2) for p in (pieces[m // 2], exchange(pieces[m // 2], 1, scen))]

    cut = PIECES - LATE
    early = edge[cut]
    top = collect(place, [group[:cut] for group in groups])
    bottom = collect(place, [group[cut:] for group in groups])
    if rows % BLOCK == 0:
        first, second = high(top, local[:early], ((0,), (0,))), high(bottom, local[early:], ((0,), (0,)))
        sums = scatter_sum_columns(place, first, second)
    else:
        first, second = high(local[:early], top, ((0,), (0,))), high(local[early:], bottom, ((0,), (0,)))
        sums = scatter_sum(first + second)
    return last(place, pieces, sums, lower)


def solution(mesh):
    in_specs = (P("scen", None, None), P("scen", None, "col"), P("scen", None), P())
    out_specs = P(("col", "scen"), None)
    return jax.shard_map(program, mesh=mesh, in_specs=in_specs, out_specs=out_specs, check_vma=False)
```

```python
import functools

import jax
import jax.numpy as jnp
from jax import lax
from jax.experimental import pallas as pl
from jax.experimental.pallas import tpu as pltpu
from jax.sharding import PartitionSpec as P


BLOCK = 128
SUB = 8


def high(left, right, dims):
    return lax.dot_general(
        left, right, (dims, ((), ())), precision=lax.Precision.HIGH, preferred_element_type=jnp.float32
    )


def full(left, right, dims):
    return lax.dot_general(
        left, right, (dims, ((), ())), precision=lax.Precision.HIGHEST, preferred_element_type=jnp.float32
    )


def eliminate(tiles):
    count, size = len(tiles), tiles[0].shape[1]
    lane = lax.broadcasted_iota(jnp.int32, (SUB, size), 1)
    sub = lax.broadcasted_iota(jnp.int32, (SUB, size), 0)

    def lanes(x, c):
        return jnp.broadcast_to(x[:, c : c + 1], (SUB, size))

    def subs(x, q):
        return jnp.broadcast_to(x[q : q + 1, :], (SUB, size))

    def row_times(columns, upper, inverse):
        raw, times = [], []
        for q in range(SUB):
            value = columns[q]
            for p in range(q):
                value = value - times[p] * upper[p, q]
            raw.append(value)
            times.append(value * inverse[q])
        return raw, times

    scaled, scales, ready = [], [], None
    for at in range(count):
        low = SUB * at
        rows = tiles[at]
        cols = ready or [lanes(rows, low + q) for q in range(SUB)]
        if at + 1 < count:
            ready = [lanes(tiles[at + 1], low + SUB + q) for q in range(SUB)]
            below = [lanes(tiles[at + 1], low + q) for q in range(SUB)]
        inverse, upper, pivots, factors = [], {}, None, []
        for q in range(SUB):
            pivot = subs(cols[q], q)
            pivots = pivot if pivots is None else jnp.where(sub == q, pivot, pivots)
            inverse.append(1.0 / pivot)
            factors.append(jnp.where(sub > q, cols[q] * inverse[q], 0.0))
            for p in range(q + 1, SUB):
                upper[q, p] = subs(cols[q], p)
                cols[p] = cols[p] - factors[q] * upper[q, p]
        if at + 1 < count:
            raw, next_times = row_times(below, upper, inverse)
            for q in range(SUB):
                for p in range(SUB):
                    ready[q] = ready[q] - next_times[p] * subs(raw[p], q)
        for q in range(SUB):
            pivot_row = jnp.where(lane == low + q, 1.0, subs(rows, q))
            rows = jnp.where((lane == low + q) & (sub > q), 0.0, rows) - factors[q] * pivot_row
        pivot_rows = []
        for q in range(SUB):
            row = jnp.where(lane == low + q, 1.0, subs(rows, q))
            pivot_rows.append(jnp.where((lane > low + q) & (lane < low + SUB), 0.0, row))
        own = (lane >= low) & (lane < low + SUB)
        for other in range(at + 1, count):
            if other == at + 1:
                times = next_times
            else:
                _, times = row_times([lanes(tiles[other], low + q) for q in range(SUB)], upper, inverse)
            tile = jnp.where(own, 0.0, tiles[other])
            for q in range(SUB):
                tile = tile - times[q] * pivot_rows[q]
            tiles[other] = tile
        scale = lax.rsqrt(pivots)
        scales.append(scale)
        scaled.append(rows * scale)
    return scaled, scales


def vmem(count):
    return [pl.BlockSpec(memory_space=pltpu.VMEM)] * count


SMEM = pl.BlockSpec(memory_space=pltpu.SMEM)


def shape(*sizes):
    return jax.ShapeDtypeStruct(sizes, jnp.float32)


def strips(nb):
    for i in range(nb // 2):
        yield i, nb - 1 - i, 0
        yield i, i, (nb - i) * BLOCK


HBM = pl.BlockSpec(memory_space=pltpu.HBM)


def split(x):
    high_part = x.astype(jnp.bfloat16)
    return high_part, (x - high_part.astype(jnp.float32)).astype(jnp.bfloat16)


def three(left, right, dims):
    def one(a, b):
        return lax.dot_general(a, b, (dims, ((), ())), preferred_element_type=jnp.float32)

    (ah, al), (bh, bl) = left, right
    return one(ah, bh) + (one(ah, bl) + one(al, bh))


def product_kernel(edges, tall, place_ref, mask_ref, inverse_hbm, coupling_hbm, *refs):
    count = len(edges) - 1
    pieces = refs[:count]
    keep_a, keep_b, send, panel, rows, ph, plo, qh, ql, rect, values, sems, out_sems = refs[count:]

    @pl.when(place_ref[0] == 0)
    def _():
        depth, width = panel.shape
        nb, steps, tile = width // BLOCK, depth // tall, depth // mask_ref.shape[1]
        copies = [pltpu.make_async_copy(coupling_hbm.at[:, pl.ds(0, width)], panel, sems.at[0])]
        for i in range(steps):
            copies.append(pltpu.make_async_copy(inverse_hbm.at[pl.ds(i * tall, tall)], rows.at[i], sems.at[1 + i]))
        for copy in copies:
            copy.start()
        stores = []
        kept = [mask_ref[0, t].astype(jnp.float32) for t in range(depth // tile)]
        copies[0].wait()
        for t in range(depth // tile):
            here = slice(t * tile, (t + 1) * tile)
            ph[here, :], plo[here, :] = split(panel[here, :] * kept[t])
        for i in range(steps):
            copies[1 + i].wait()
            value = three(split(rows[i]), (ph[...], plo[...]), ((1,), (0,)))
            for t in range(i * tall // tile, (i + 1) * tall // tile):
                part = value[t * tile - i * tall : (t + 1) * tile - i * tall, :] * kept[t]
                here = slice(t * tile, (t + 1) * tile)
                qh[here, :], ql[here, :] = split(part)
                values[here, :] = part
            for k in range(count):
                if i * tall < edges[k + 1] <= (i + 1) * tall:
                    mine = pl.ds(edges[k], edges[k + 1] - edges[k])
                    stores.append(pltpu.make_async_copy(values.at[mine], pieces[k], out_sems.at[k]))
                    stores[-1].start()
        for i, block, low in strips(nb):
            wide = (block + 1) * BLOCK
            mine = slice(block * BLOCK, wide)
            rect[i * BLOCK : (i + 1) * BLOCK, low : low + wide] = three(
                (ph[:, mine], plo[:, mine]), (qh[:, :wide], ql[:, :wide]), ((0,), (0,))
            )
        half = rect.shape[0] // 2
        core = place_ref[1] & 1
        mine = pl.multiple_of(core * half, half)
        theirs = pl.multiple_of((1 - core) * half, half)
        keep_a[...] = rect[pl.ds(mine, half // 2), :]
        keep_b[...] = rect[pl.ds(mine + half // 2, half // 2), :]
        send[...] = rect[pl.ds(theirs, half), :]
        for store in stores:
            store.wait()


def product(place, mask, inverse, coupling, width, edges):
    depth, count = inverse.shape[0], len(edges) - 1
    nb, tall = width // BLOCK, depth // 4
    high_rows, wide = nb // 2 * BLOCK, (nb + 1) * BLOCK
    return pl.pallas_call(
        functools.partial(product_kernel, edges, tall),
        out_shape=tuple(shape(b - a, width) for a, b in zip(edges, edges[1:]))
        + (shape(high_rows // 4, wide), shape(high_rows // 4, wide), shape(high_rows // 2, wide)),
        in_specs=[SMEM, SMEM, HBM, HBM],
        out_specs=tuple([HBM] * count + vmem(3)),
        scratch_shapes=[pltpu.VMEM((depth, width), jnp.float32), pltpu.VMEM((depth // tall, tall, depth), jnp.float32)]
        + [pltpu.VMEM((depth, width), jnp.bfloat16)] * 4
        + [pltpu.VMEM((high_rows, wide), jnp.float32), pltpu.VMEM((depth, width), jnp.float32)]
        + [pltpu.SemaphoreType.DMA((1 + depth // tall,)), pltpu.SemaphoreType.DMA((count,))],
        compiler_params=pltpu.CompilerParams(vmem_limit_bytes=61 << 20),
        cost_estimate=pl.CostEstimate(
            flops=6 * depth * width * (depth + width), bytes_accessed=4 * depth * (depth + 2 * width), transcendentals=0
        ),
    )(place, mask, inverse, coupling)


def collect_kernel(planes, count, place_ref, *refs):
    groups, (out_ref, sems) = refs[: planes * count], refs[planes * count :]
    for h in range(planes):

        @pl.when(place_ref[0] == h)
        def _(h=h):
            low, copies = 0, []
            for k in range(count):
                ref = groups[h * count + k]
                copies.append(pltpu.make_async_copy(ref, out_ref.at[pl.ds(low, ref.shape[0])], sems.at[k]))
                low += ref.shape[0]
            for copy in copies:
                copy.start()
            for copy in copies:
                copy.wait()


def collect(place, groups):
    count = len(groups[0])
    rows, width = sum(x.shape[0] for x in groups[0]), groups[0][0].shape[1]
    return pl.pallas_call(
        functools.partial(collect_kernel, len(groups), count),
        out_shape=shape(rows, width),
        in_specs=[SMEM] + [pl.BlockSpec(memory_space=pl.ANY)] * (len(groups) * count),
        out_specs=vmem(1)[0],
        scratch_shapes=[pltpu.SemaphoreType.DMA((count,))],
        compiler_params=pltpu.CompilerParams(vmem_limit_bytes=8 << 20),
        cost_estimate=pl.CostEstimate(flops=0, bytes_accessed=8 * rows * width, transcendentals=0),
    )(place, *[x for group in groups for x in group])


def part_kernel(planes, place_ref, first_ref, local_hbm, *refs):
    pieces, (keep_ref, send_ref, piece_ref, local_ref, sems) = refs[:planes], refs[planes:]
    late, wide = piece_ref.shape[0], keep_ref.shape[2]
    depth = local_hbm.shape[0]
    bring = pltpu.make_async_copy(local_hbm.at[pl.ds(depth - late, late)], local_ref, sems.at[0])
    bring.start()
    for h in range(planes):

        @pl.when(place_ref[0] == h)
        def _(h=h):
            copy = pltpu.make_async_copy(pieces[h], piece_ref, sems.at[1])
            copy.start()
            copy.wait()

    bring.wait()
    core = place_ref[1] & 1
    left = split(piece_ref[...])
    for ref, bit in ((send_ref, 1 - core), (keep_ref, core)):
        for j in range(ref.shape[0]):
            here = pl.ds(pl.multiple_of((2 * j + bit) * wide, wide), wide)
            ref[j] = first_ref[:, here] + three(left, split(local_ref[:, here]), ((0,), (0,)))


def part(place, first, local, pieces, scen):
    width, cols = first.shape
    late = pieces[0].shape[0]
    half = shape(scen // 2, width, cols // scen)
    return pl.pallas_call(
        functools.partial(part_kernel, len(pieces)),
        out_shape=(half, half),
        in_specs=[SMEM] + vmem(1) + [HBM] + [pl.BlockSpec(memory_space=pl.ANY)] * len(pieces),
        out_specs=tuple(vmem(2)),
        scratch_shapes=[
            pltpu.VMEM((late, width), jnp.float32),
            pltpu.VMEM((late, cols), jnp.float32),
            pltpu.SemaphoreType.DMA((2,)),
        ],
        compiler_params=pltpu.CompilerParams(vmem_limit_bytes=16 << 20),
        cost_estimate=pl.CostEstimate(flops=6 * late * width * cols, bytes_accessed=8 * width * cols, transcendentals=0),
    )(place, first, local, *pieces)


def turn_kernel(cuts, place_ref, own_ref, got_ref, *outs):
    for (low, high_row, position, bit), keep_ref, send_ref in zip(cuts, outs[::2], outs[1::2]):
        mine = (place_ref[1] >> bit) & 1
        rows = slice(low, high_row)
        for ref, value in ((keep_ref, mine), (send_ref, 1 - mine)):
            for j in range(ref.shape[0]):
                at = ((j >> position) << (position + 1)) + (j & ((1 << position) - 1)) + (value << position)
                ref[j] = own_ref[at, rows, :] + got_ref[at, rows, :]


def turn(place, own, got, cuts):
    blocks, _, wide = own.shape
    outs = tuple(shape(blocks // 2, high_row - low, wide) for low, high_row, _, _ in cuts for _ in range(2))
    return pl.pallas_call(
        functools.partial(turn_kernel, cuts),
        out_shape=outs,
        in_specs=[SMEM] + vmem(2),
        out_specs=tuple(vmem(len(outs))),
        compiler_params=pltpu.CompilerParams(vmem_limit_bytes=12 << 20),
        cost_estimate=pl.CostEstimate(flops=own.size, bytes_accessed=12 * own.size, transcendentals=0),
    )(place, own, got)


def factor_kernel(place_ref, own_a, own_b, other_a, other_b, diag_ref, own_ref, piece_ref, l_ref, w_ref, rect_ref, base_ref, scale_ref):
    size = w_ref.shape[0]
    nb = size // BLOCK
    plane, me = place_ref[0], place_ref[1]

    @pl.when(plane == 0)
    def _():
        half = rect_ref.shape[0] // 2
        quarter = half // 2
        core = me & 1
        mine = pl.multiple_of(core * half, half)
        theirs = pl.multiple_of((1 - core) * half, half)
        rect_ref[pl.ds(mine, quarter), :] = own_a[...]
        rect_ref[pl.ds(mine + quarter, quarter), :] = own_b[...]
        rect_ref[pl.ds(theirs, quarter), :] = other_a[...]
        rect_ref[pl.ds(theirs + quarter, quarter), :] = other_b[...]
        row = lax.broadcasted_iota(jnp.int32, (BLOCK, BLOCK), 0)
        col = lax.broadcasted_iota(jnp.int32, (BLOCK, BLOCK), 1)
        for i, block, low in strips(nb):
            here = slice(block * BLOCK, (block + 1) * BLOCK)
            for k in range(block + 1):
                there = slice(k * BLOCK, (k + 1) * BLOCK)
                part = rect_ref[i * BLOCK : (i + 1) * BLOCK, low + k * BLOCK : low + (k + 1) * BLOCK]
                if k == block:
                    part = jnp.where(col <= row, part, part.T)
                    part = part + jnp.where(col == row, diag_ref[:, here], 0.0)
                w_ref[here, there] = part

        def nt(left, right):
            return full(left, right, ((1,), (1,)))

        def nn(left, right):
            return full(left, right, ((1,), (0,)))

        for j in range(nb):
            low, top = j * BLOCK, (j + 1) * BLOCK
            mine = slice(low, top)
            scaled, scales = eliminate([w_ref[low + SUB * t : low + SUB * (t + 1), mine] for t in range(BLOCK // SUB)])
            for t in range(BLOCK // SUB):
                base_ref[SUB * t : SUB * t + SUB, :] = scaled[t]
                scale_ref[SUB * t : SUB * t + SUB, :] = scales[t]
            both = base_ref[...]
            inverse = jnp.where(col < row, both, jnp.where(col == row, scale_ref[...], 0.0))
            l_ref[mine, mine] = jnp.where(col >= row, both, 0.0).T
            if top < size:
                l_ref[mine, top:] = jnp.zeros((BLOCK, size - top), jnp.float32)
            if j:
                w_ref[mine, :low] = nn(inverse, w_ref[mine, :low])
            w_ref[mine, mine] = inverse
            if top < size:
                panel = nt(w_ref[top:, mine], inverse)
                l_ref[top:, mine] = panel
                for k in range(j + 1, nb):
                    here, skip = slice(k * BLOCK, (k + 1) * BLOCK), (k - j - 1) * BLOCK
                    w_ref[k * BLOCK :, here] = w_ref[k * BLOCK :, here] - nt(panel[skip:], panel[skip : skip + BLOCK])
                if j:
                    w_ref[top:, :low] = w_ref[top:, :low] - nn(panel, w_ref[mine, :low])
                w_ref[top:, mine] = -nn(panel, inverse)
        for i, block, low in strips(nb):
            for k in range(block + 1):
                rect_ref[i * BLOCK : (i + 1) * BLOCK, low + k * BLOCK : low + (k + 1) * BLOCK] = w_ref[
                    block * BLOCK : (block + 1) * BLOCK, k * BLOCK : (k + 1) * BLOCK
                ]
        rows = own_ref.shape[0]
        first = jnp.minimum(place_ref[2], size - rows)
        own_ref[...] = l_ref[pl.ds(pl.multiple_of(first, rows), rows), :]
        each = piece_ref.shape[0]
        piece_ref[...] = rect_ref[pl.ds(pl.multiple_of(me * each, each), each), :]


def factor(place, parts, diag, each, rows):
    size = diag.shape[1]
    nb = size // BLOCK
    tall, wide = nb // 2 * BLOCK, (nb + 1) * BLOCK
    return pl.pallas_call(
        factor_kernel,
        out_shape=(shape(rows, size), shape(each, wide)),
        in_specs=[SMEM] + vmem(5),
        out_specs=tuple(vmem(2)),
        scratch_shapes=[
            pltpu.VMEM((size, size), jnp.float32),
            pltpu.VMEM((size, size), jnp.float32),
            pltpu.VMEM((tall, wide), jnp.float32),
            pltpu.VMEM((BLOCK, BLOCK), jnp.float32),
            pltpu.VMEM((BLOCK, BLOCK), jnp.float32),
        ],
        compiler_params=pltpu.CompilerParams(vmem_limit_bytes=16 << 20),
        cost_estimate=pl.CostEstimate(flops=20 * size**3, bytes_accessed=12 * size * size, transcendentals=size),
    )(place, *parts, diag)


def last_kernel(count, place_ref, *refs):
    pieces, (keep_a, got_a, keep_b, got_b, own_ref, out_ref, rect_ref, rows_ref) = refs[:count], refs[count:]
    me, first = place_ref[1], place_ref[2]
    rows, width = out_ref.shape
    nb = width // BLOCK
    each = pieces[0].shape[0]
    if len(keep_a.shape) == 3:
        half = keep_a.shape[1]
        rows_ref[:, :half] = (keep_a[0] + got_a[0]).T
        rows_ref[:, half:] = (keep_b[0] + got_b[0]).T
    else:
        half = rows // 2
        rows_ref[:half, :] = keep_a[...] + got_a[...]
        rows_ref[half:, :] = keep_b[...] + got_b[...]
    for m in range(count):
        rect_ref[pl.ds(pl.multiple_of((me ^ m) * each, each), each), :] = pieces[m][...]
    for i, block, low in strips(nb):
        wide = (block + 1) * BLOCK
        part = rect_ref[i * BLOCK : (i + 1) * BLOCK, low : low + wide]
        part = jnp.concatenate(
            [part[:, : wide - BLOCK], jnp.where(
                lax.broadcasted_iota(jnp.int32, (BLOCK, BLOCK), 1) <= lax.broadcasted_iota(jnp.int32, (BLOCK, BLOCK), 0),
                part[:, wide - BLOCK :], 0.0)], axis=1) if wide > BLOCK else part
        out_ref[:, block * BLOCK : (block + 1) * BLOCK] = three(split(rows_ref[:, :wide]), split(part), ((1,), (1,)))

    @pl.when(first < width)
    def _():
        out_ref[...] = own_ref[...]


def last(place, pieces, sums, own):
    rows, width = own.shape
    nb = width // BLOCK
    tall, wide = nb // 2 * BLOCK, (nb + 1) * BLOCK
    return pl.pallas_call(
        functools.partial(last_kernel, len(pieces)),
        out_shape=shape(rows, width),
        in_specs=[SMEM] + vmem(len(pieces) + 5),
        out_specs=vmem(1)[0],
        scratch_shapes=[pltpu.VMEM((tall, wide), jnp.float32), pltpu.VMEM((rows, width), jnp.float32)],
        compiler_params=pltpu.CompilerParams(vmem_limit_bytes=12 << 20),
        cost_estimate=pl.CostEstimate(flops=6 * rows * width * width, bytes_accessed=8 * width * width, transcendentals=0),
    )(place, *pieces, *sums, own)


def hop(x, source, target):
    return lax.ppermute(x, "col", [(source, target)])


def exchange(x, mask, count):
    return lax.ppermute(x, "scen", [(i, i ^ mask) for i in range(count)])


def orders(count):
    bits = count.bit_length() - 1
    split = 1 + bits // 2
    return bits, list(range(1, split)), list(range(split, bits))


def halve(x, names, bit, count):
    axis = names.index(bit)
    mine = (lax.axis_index("scen") >> bit) & 1
    keep = lax.dynamic_index_in_dim(x, mine, axis, keepdims=False)
    send = lax.dynamic_index_in_dim(x, 1 - mine, axis, keepdims=False)
    return keep, exchange(send, 1 << bit, count), [n for n in names if n != bit]


def scatter_sum(x):
    count = lax.axis_size("scen")
    bits, first, second = orders(count)
    rows = x.shape[0] // count
    x = x.reshape((2,) * bits + (rows,) + x.shape[1:])
    keep, got, names = halve(x, list(range(bits - 1, -1, -1)), 0, count)
    x = keep + got
    lead = (slice(None),) * len(names)
    parts = [x[lead + (slice(0, rows // 2),)], x[lead + (slice(rows // 2, rows),)]]
    lists, pairs = [names, names], [None, None]
    for a, b in zip(first + second, second + first):
        for i, bit in ((0, a), (1, b)):
            if pairs[i] is not None:
                parts[i] = pairs[i][0] + pairs[i][1]
            keep, got, lists[i] = halve(parts[i], lists[i], bit, count)
            pairs[i] = (keep, got)
    return pairs[0] + pairs[1]


def scatter_sum_columns(place, first, local, pieces):
    count = lax.axis_size("scen")
    bits, near, far = orders(count)
    half = first.shape[0] // 2
    keep, send = part(place, first, local, pieces, count)
    got = exchange(send, 1, count)
    left = [list(range(1, bits)), list(range(1, bits))]
    pairs = None
    for a, b in zip(near + far, far + near):
        if pairs is None:
            cuts = tuple((i * half, (i + 1) * half, left[i].index(bit), bit) for i, bit in ((0, a), (1, b)))
            outs = turn(place, keep, got, cuts)
        else:
            outs = ()
            for i, bit in ((0, a), (1, b)):
                outs += turn(place, *pairs[i], ((0, half, left[i].index(bit), bit),))
        pairs = []
        for i, bit in ((0, a), (1, b)):
            left[i].remove(bit)
            pairs.append((outs[2 * i], exchange(outs[2 * i + 1], 1 << bit, count)))
    return pairs[0] + pairs[1]


PIECES = 8
LATE = 1


def bounds(depth):
    units = depth // (2 * SUB)
    return [units * k // PIECES * 2 * SUB for k in range(PIECES + 1)]


def program(inverses, coupling, tile_mask, hess_diag):
    local = coupling[0]
    width = hess_diag.shape[0]
    scen, planes = lax.axis_size("scen"), lax.axis_size("col")
    me, plane = lax.axis_index("scen").astype(jnp.int32), lax.axis_index("col").astype(jnp.int32)
    rows = local.shape[1] // scen
    place = jnp.stack([plane, me, plane * local.shape[1] + me * rows])
    edge = bounds(local.shape[0])

    *own, keep_a, keep_b, send = product(place, tile_mask, inverses[0], local, width, edge)

    groups = [own]
    for h in range(planes - 1):
        groups.append([hop(groups[h][k], h, h + 1) for k in range(PIECES)])

    got = exchange(send, 1, scen)
    a, b = keep_a + got[: got.shape[0] // 2], keep_b + got[got.shape[0] // 2 :]
    _, near, far = orders(scen)
    for p, q in zip(near + far, far + near):
        got_a = exchange(a, 1 << p, scen)
        got_b = exchange(b, 1 << q, scen)
        a, b = a + got_a, b + got_b
    parts = (a, b, exchange(a, 1, scen), exchange(b, 1, scen))
    each = width // BLOCK // 2 * BLOCK // scen
    lower, piece = factor(place, parts, hess_diag[None, :], each, rows)

    mine = jnp.where(plane == 0, piece, 0.0)
    for h in range(1, planes):
        piece = hop(piece, h - 1, h)
        mine = mine + piece
    pieces = [mine if m == 0 else exchange(mine, m, scen) for m in range(0, scen, 2)]
    pieces = [p for m in range(0, scen, 2) for p in (pieces[m // 2], exchange(pieces[m // 2], 1, scen))]

    cut = PIECES - LATE
    early = edge[cut]
    top = collect(place, [group[:cut] for group in groups])
    if rows % BLOCK == 0:
        first = high(top, local[:early], ((0,), (0,)))
        sums = scatter_sum_columns(place, first, local, [group[cut] for group in groups])
    else:
        bottom = collect(place, [group[cut:] for group in groups])
        first, second = high(local[:early], top, ((0,), (0,))), high(local[early:], bottom, ((0,), (0,)))
        sums = scatter_sum(first + second)
    return last(place, pieces, sums, lower)


def solution(mesh):
    in_specs = (P("scen", None, None), P("scen", None, "col"), P("scen", None), P())
    out_specs = P(("col", "scen"), None)
    return jax.shard_map(program, mesh=mesh, in_specs=in_specs, out_specs=out_specs, check_vma=False)
```

```python
import functools

import jax
import jax.numpy as jnp
from jax import lax
from jax.experimental import pallas as pl
from jax.experimental.pallas import tpu as pltpu
from jax.sharding import PartitionSpec as P


BLOCK = 128
SUB = 8


def high(left, right, dims):
    return lax.dot_general(
        left, right, (dims, ((), ())), precision=lax.Precision.HIGH, preferred_element_type=jnp.float32
    )


def full(left, right, dims):
    return lax.dot_general(
        left, right, (dims, ((), ())), precision=lax.Precision.HIGHEST, preferred_element_type=jnp.float32
    )


def eliminate(tiles):
    count, size = len(tiles), tiles[0].shape[1]
    lane = lax.broadcasted_iota(jnp.int32, (SUB, size), 1)
    sub = lax.broadcasted_iota(jnp.int32, (SUB, size), 0)

    def lanes(x, c):
        return jnp.broadcast_to(x[:, c : c + 1], (SUB, size))

    def subs(x, q):
        return jnp.broadcast_to(x[q : q + 1, :], (SUB, size))

    def row_times(columns, upper, inverse):
        raw, times = [], []
        for q in range(SUB):
            value = columns[q]
            for p in range(q):
                value = value - times[p] * upper[p, q]
            raw.append(value)
            times.append(value * inverse[q])
        return raw, times

    scaled, scales, ready = [], [], None
    for at in range(count):
        low = SUB * at
        rows = tiles[at]
        cols = ready or [lanes(rows, low + q) for q in range(SUB)]
        if at + 1 < count:
            ready = [lanes(tiles[at + 1], low + SUB + q) for q in range(SUB)]
            below = [lanes(tiles[at + 1], low + q) for q in range(SUB)]
        inverse, upper, pivots, factors = [], {}, None, []
        for q in range(SUB):
            pivot = subs(cols[q], q)
            pivots = pivot if pivots is None else jnp.where(sub == q, pivot, pivots)
            inverse.append(1.0 / pivot)
            factors.append(jnp.where(sub > q, cols[q] * inverse[q], 0.0))
            for p in range(q + 1, SUB):
                upper[q, p] = subs(cols[q], p)
                cols[p] = cols[p] - factors[q] * upper[q, p]
        if at + 1 < count:
            raw, next_times = row_times(below, upper, inverse)
            for q in range(SUB):
                for p in range(SUB):
                    ready[q] = ready[q] - next_times[p] * subs(raw[p], q)
        for q in range(SUB):
            pivot_row = jnp.where(lane == low + q, 1.0, subs(rows, q))
            rows = jnp.where((lane == low + q) & (sub > q), 0.0, rows) - factors[q] * pivot_row
        pivot_rows = []
        for q in range(SUB):
            row = jnp.where(lane == low + q, 1.0, subs(rows, q))
            pivot_rows.append(jnp.where((lane > low + q) & (lane < low + SUB), 0.0, row))
        own = (lane >= low) & (lane < low + SUB)
        for other in range(at + 1, count):
            if other == at + 1:
                times = next_times
            else:
                _, times = row_times([lanes(tiles[other], low + q) for q in range(SUB)], upper, inverse)
            tile = jnp.where(own, 0.0, tiles[other])
            for q in range(SUB):
                tile = tile - times[q] * pivot_rows[q]
            tiles[other] = tile
        scale = lax.rsqrt(pivots)
        scales.append(scale)
        scaled.append(rows * scale)
    return scaled, scales


def vmem(count):
    return [pl.BlockSpec(memory_space=pltpu.VMEM)] * count


SMEM = pl.BlockSpec(memory_space=pltpu.SMEM)


def shape(*sizes):
    return jax.ShapeDtypeStruct(sizes, jnp.float32)


def strips(nb):
    for i in range(nb // 2):
        yield i, nb - 1 - i, 0
        yield i, i, (nb - i) * BLOCK


HBM = pl.BlockSpec(memory_space=pltpu.HBM)


def split(x):
    high_part = x.astype(jnp.bfloat16)
    return high_part, (x - high_part.astype(jnp.float32)).astype(jnp.bfloat16)


def three(left, right, dims):
    def one(a, b):
        return lax.dot_general(a, b, (dims, ((), ())), preferred_element_type=jnp.float32)

    (ah, al), (bh, bl) = left, right
    return one(ah, bh) + (one(ah, bl) + one(al, bh))


def product_kernel(edges, start, stop, tall, place_ref, mask_ref, inverse_hbm, coupling_hbm, *refs):
    given = [k for k in range(len(edges) - 1) if edges[k + 1] <= start]
    made = [k for k in range(len(edges) - 1) if start <= edges[k] and edges[k + 1] <= stop]
    earlier, refs = refs[: len(given)], refs[len(given) :]
    pieces, refs = dict(zip(made, refs)), refs[len(made) :]
    corner, (panel, rows, ph, plo, qh, ql, rect, values, sems, out_sems) = refs[:-10], refs[-10:]

    @pl.when(place_ref[0] == 0)
    def _():
        depth, width = panel.shape
        nb, tile = width // BLOCK, depth // mask_ref.shape[1]
        bring = pltpu.make_async_copy(coupling_hbm.at[:, pl.ds(0, width)], panel, sems.at[0])
        bring.start()
        copies = []
        for i in range(start // tall, stop // tall):
            copies.append(pltpu.make_async_copy(inverse_hbm.at[pl.ds(i * tall, tall)], rows.at[i], sems.at[1 + i]))
            copies[-1].start()
        back = []
        for k, ref in zip(given, earlier):
            mine = pl.ds(edges[k], edges[k + 1] - edges[k])
            back.append(pltpu.make_async_copy(ref, values.at[mine], out_sems.at[k]))
            back[-1].start()
        kept = [mask_ref[0, t].astype(jnp.float32) for t in range(depth // tile)]
        bring.wait()
        for t in range(depth // tile):
            here = slice(t * tile, (t + 1) * tile)
            ph[here, :], plo[here, :] = split(panel[here, :] * kept[t])
        stores = []
        for i, copy in zip(range(start // tall, stop // tall), copies):
            copy.wait()
            value = three(split(rows[i]), (ph[...], plo[...]), ((1,), (0,)))
            for t in range(i * tall // tile, (i + 1) * tall // tile):
                part = value[t * tile - i * tall : (t + 1) * tile - i * tall, :] * kept[t]
                here = slice(t * tile, (t + 1) * tile)
                if corner:
                    qh[here, :], ql[here, :] = split(part)
                values[here, :] = part
            for k in made:
                if i * tall < edges[k + 1] <= (i + 1) * tall:
                    mine = pl.ds(edges[k], edges[k + 1] - edges[k])
                    stores.append(pltpu.make_async_copy(values.at[mine], pieces[k], out_sems.at[k]))
                    stores[-1].start()
        for k, copy in zip(given, back):
            copy.wait()
            here = slice(edges[k], edges[k + 1])
            qh[here, :], ql[here, :] = split(values[here, :])
        if corner:
            keep_a, keep_b, send = corner
            for i, block, low in strips(nb):
                wide = (block + 1) * BLOCK
                mine = slice(block * BLOCK, wide)
                rect[i * BLOCK : (i + 1) * BLOCK, low : low + wide] = three(
                    (ph[:, mine], plo[:, mine]), (qh[:, :wide], ql[:, :wide]), ((0,), (0,))
                )
            half = rect.shape[0] // 2
            core = place_ref[1] & 1
            mine = pl.multiple_of(core * half, half)
            theirs = pl.multiple_of((1 - core) * half, half)
            keep_a[...] = rect[pl.ds(mine, half // 2), :]
            keep_b[...] = rect[pl.ds(mine + half // 2, half // 2), :]
            send[...] = rect[pl.ds(theirs, half), :]
        for store in stores:
            store.wait()


def product(place, mask, inverse, coupling, width, edges, start, stop, earlier):
    depth, count = inverse.shape[0], len(edges) - 1
    nb, tall = width // BLOCK, edges[HEAD]
    high_rows, wide = nb // 2 * BLOCK, (nb + 1) * BLOCK
    made = [shape(b - a, width) for a, b in zip(edges, edges[1:]) if start <= a and b <= stop]
    corner = [shape(high_rows // 4, wide), shape(high_rows // 4, wide), shape(high_rows // 2, wide)]
    corner = corner if stop == depth else []
    return pl.pallas_call(
        functools.partial(product_kernel, edges, start, stop, tall),
        out_shape=tuple(made + corner),
        in_specs=[SMEM, SMEM, HBM, HBM] + [HBM] * len(earlier),
        out_specs=tuple([HBM] * len(made) + vmem(len(corner))),
        scratch_shapes=[pltpu.VMEM((depth, width), jnp.float32), pltpu.VMEM((depth // tall, tall, depth), jnp.float32)]
        + [pltpu.VMEM((depth, width), jnp.bfloat16)] * 4
        + [pltpu.VMEM((high_rows, wide), jnp.float32), pltpu.VMEM((depth, width), jnp.float32)]
        + [pltpu.SemaphoreType.DMA((1 + depth // tall,)), pltpu.SemaphoreType.DMA((count,))],
        compiler_params=pltpu.CompilerParams(vmem_limit_bytes=61 << 20),
        cost_estimate=pl.CostEstimate(
            flops=6 * depth * width * (stop - start), bytes_accessed=4 * depth * (depth + 2 * width), transcendentals=0
        ),
    )(place, mask, inverse, coupling, *earlier)


def collect_kernel(planes, count, place_ref, *refs):
    groups, (out_ref, sems) = refs[: planes * count], refs[planes * count :]
    for h in range(planes):

        @pl.when(place_ref[0] == h)
        def _(h=h):
            low, copies = 0, []
            for k in range(count):
                ref = groups[h * count + k]
                copies.append(pltpu.make_async_copy(ref, out_ref.at[pl.ds(low, ref.shape[0])], sems.at[k]))
                low += ref.shape[0]
            for copy in copies:
                copy.start()
            for copy in copies:
                copy.wait()


def collect(place, groups):
    count = len(groups[0])
    rows, width = sum(x.shape[0] for x in groups[0]), groups[0][0].shape[1]
    return pl.pallas_call(
        functools.partial(collect_kernel, len(groups), count),
        out_shape=shape(rows, width),
        in_specs=[SMEM] + [pl.BlockSpec(memory_space=pl.ANY)] * (len(groups) * count),
        out_specs=vmem(1)[0],
        scratch_shapes=[pltpu.SemaphoreType.DMA((count,))],
        compiler_params=pltpu.CompilerParams(vmem_limit_bytes=8 << 20),
        cost_estimate=pl.CostEstimate(flops=0, bytes_accessed=8 * rows * width, transcendentals=0),
    )(place, *[x for group in groups for x in group])


def part_kernel(planes, place_ref, first_ref, local_hbm, *refs):
    pieces, (keep_ref, send_ref, piece_ref, local_ref, sems) = refs[:planes], refs[planes:]
    late, wide = piece_ref.shape[0], keep_ref.shape[2]
    depth = local_hbm.shape[0]
    bring = pltpu.make_async_copy(local_hbm.at[pl.ds(depth - late, late)], local_ref, sems.at[0])
    bring.start()
    for h in range(planes):

        @pl.when(place_ref[0] == h)
        def _(h=h):
            copy = pltpu.make_async_copy(pieces[h], piece_ref, sems.at[1])
            copy.start()
            copy.wait()

    bring.wait()
    core = place_ref[1] & 1
    left = split(piece_ref[...])
    for ref, bit in ((send_ref, 1 - core), (keep_ref, core)):
        for j in range(ref.shape[0]):
            here = pl.ds(pl.multiple_of((2 * j + bit) * wide, wide), wide)
            ref[j] = first_ref[:, here] + three(left, split(local_ref[:, here]), ((0,), (0,)))


def part(place, first, local, pieces, scen):
    width, cols = first.shape
    late = pieces[0].shape[0]
    half = shape(scen // 2, width, cols // scen)
    return pl.pallas_call(
        functools.partial(part_kernel, len(pieces)),
        out_shape=(half, half),
        in_specs=[SMEM] + vmem(1) + [HBM] + [pl.BlockSpec(memory_space=pl.ANY)] * len(pieces),
        out_specs=tuple(vmem(2)),
        scratch_shapes=[
            pltpu.VMEM((late, width), jnp.float32),
            pltpu.VMEM((late, cols), jnp.float32),
            pltpu.SemaphoreType.DMA((2,)),
        ],
        compiler_params=pltpu.CompilerParams(vmem_limit_bytes=16 << 20),
        cost_estimate=pl.CostEstimate(flops=6 * late * width * cols, bytes_accessed=8 * width * cols, transcendentals=0),
    )(place, first, local, *pieces)


def turn_kernel(cuts, place_ref, own_ref, got_ref, *outs):
    for (low, high_row, position, bit), keep_ref, send_ref in zip(cuts, outs[::2], outs[1::2]):
        mine = (place_ref[1] >> bit) & 1
        rows = slice(low, high_row)
        for ref, value in ((keep_ref, mine), (send_ref, 1 - mine)):
            for j in range(ref.shape[0]):
                at = ((j >> position) << (position + 1)) + (j & ((1 << position) - 1)) + (value << position)
                ref[j] = own_ref[at, rows, :] + got_ref[at, rows, :]


def turn(place, own, got, cuts):
    blocks, _, wide = own.shape
    outs = tuple(shape(blocks // 2, high_row - low, wide) for low, high_row, _, _ in cuts for _ in range(2))
    return pl.pallas_call(
        functools.partial(turn_kernel, cuts),
        out_shape=outs,
        in_specs=[SMEM] + vmem(2),
        out_specs=tuple(vmem(len(outs))),
        compiler_params=pltpu.CompilerParams(vmem_limit_bytes=12 << 20),
        cost_estimate=pl.CostEstimate(flops=own.size, bytes_accessed=12 * own.size, transcendentals=0),
    )(place, own, got)


def factor_kernel(place_ref, own_a, own_b, other_a, other_b, diag_ref, own_ref, piece_ref, l_ref, w_ref, rect_ref, base_ref, scale_ref):
    size = w_ref.shape[0]
    nb = size // BLOCK
    plane, me = place_ref[0], place_ref[1]

    @pl.when(plane == 0)
    def _():
        half = rect_ref.shape[0] // 2
        quarter = half // 2
        core = me & 1
        mine = pl.multiple_of(core * half, half)
        theirs = pl.multiple_of((1 - core) * half, half)
        rect_ref[pl.ds(mine, quarter), :] = own_a[...]
        rect_ref[pl.ds(mine + quarter, quarter), :] = own_b[...]
        rect_ref[pl.ds(theirs, quarter), :] = other_a[...]
        rect_ref[pl.ds(theirs + quarter, quarter), :] = other_b[...]
        row = lax.broadcasted_iota(jnp.int32, (BLOCK, BLOCK), 0)
        col = lax.broadcasted_iota(jnp.int32, (BLOCK, BLOCK), 1)
        for i, block, low in strips(nb):
            here = slice(block * BLOCK, (block + 1) * BLOCK)
            for k in range(block + 1):
                there = slice(k * BLOCK, (k + 1) * BLOCK)
                part = rect_ref[i * BLOCK : (i + 1) * BLOCK, low + k * BLOCK : low + (k + 1) * BLOCK]
                if k == block:
                    part = jnp.where(col <= row, part, part.T)
                    part = part + jnp.where(col == row, diag_ref[:, here], 0.0)
                w_ref[here, there] = part

        def nt(left, right):
            return full(left, right, ((1,), (1,)))

        def nn(left, right):
            return full(left, right, ((1,), (0,)))

        for j in range(nb):
            low, top = j * BLOCK, (j + 1) * BLOCK
            mine = slice(low, top)
            scaled, scales = eliminate([w_ref[low + SUB * t : low + SUB * (t + 1), mine] for t in range(BLOCK // SUB)])
            for t in range(BLOCK // SUB):
                base_ref[SUB * t : SUB * t + SUB, :] = scaled[t]
                scale_ref[SUB * t : SUB * t + SUB, :] = scales[t]
            both = base_ref[...]
            inverse = jnp.where(col < row, both, jnp.where(col == row, scale_ref[...], 0.0))
            l_ref[mine, mine] = jnp.where(col >= row, both, 0.0).T
            if top < size:
                l_ref[mine, top:] = jnp.zeros((BLOCK, size - top), jnp.float32)
            if j:
                w_ref[mine, :low] = nn(inverse, w_ref[mine, :low])
            w_ref[mine, mine] = inverse
            if top < size:
                panel = nt(w_ref[top:, mine], inverse)
                l_ref[top:, mine] = panel
                for k in range(j + 1, nb):
                    here, skip = slice(k * BLOCK, (k + 1) * BLOCK), (k - j - 1) * BLOCK
                    w_ref[k * BLOCK :, here] = w_ref[k * BLOCK :, here] - nt(panel[skip:], panel[skip : skip + BLOCK])
                if j:
                    w_ref[top:, :low] = w_ref[top:, :low] - nn(panel, w_ref[mine, :low])
                w_ref[top:, mine] = -nn(panel, inverse)
        for i, block, low in strips(nb):
            for k in range(block + 1):
                rect_ref[i * BLOCK : (i + 1) * BLOCK, low + k * BLOCK : low + (k + 1) * BLOCK] = w_ref[
                    block * BLOCK : (block + 1) * BLOCK, k * BLOCK : (k + 1) * BLOCK
                ]
        rows = own_ref.shape[0]
        first = jnp.minimum(place_ref[2], size - rows)
        own_ref[...] = l_ref[pl.ds(pl.multiple_of(first, rows), rows), :]
        each = piece_ref.shape[0]
        piece_ref[...] = rect_ref[pl.ds(pl.multiple_of(me * each, each), each), :]


def factor(place, parts, diag, each, rows):
    size = diag.shape[1]
    nb = size // BLOCK
    tall, wide = nb // 2 * BLOCK, (nb + 1) * BLOCK
    return pl.pallas_call(
        factor_kernel,
        out_shape=(shape(rows, size), shape(each, wide)),
        in_specs=[SMEM] + vmem(5),
        out_specs=tuple(vmem(2)),
        scratch_shapes=[
            pltpu.VMEM((size, size), jnp.float32),
            pltpu.VMEM((size, size), jnp.float32),
            pltpu.VMEM((tall, wide), jnp.float32),
            pltpu.VMEM((BLOCK, BLOCK), jnp.float32),
            pltpu.VMEM((BLOCK, BLOCK), jnp.float32),
        ],
        compiler_params=pltpu.CompilerParams(vmem_limit_bytes=16 << 20),
        cost_estimate=pl.CostEstimate(flops=20 * size**3, bytes_accessed=12 * size * size, transcendentals=size),
    )(place, *parts, diag)


def last_kernel(count, place_ref, *refs):
    pieces, (keep_a, got_a, keep_b, got_b, own_ref, out_ref, rect_ref, rows_ref) = refs[:count], refs[count:]
    me, first = place_ref[1], place_ref[2]
    rows, width = out_ref.shape
    nb = width // BLOCK
    each = pieces[0].shape[0]
    if len(keep_a.shape) == 3:
        half = keep_a.shape[1]
        rows_ref[:, :half] = (keep_a[0] + got_a[0]).T
        rows_ref[:, half:] = (keep_b[0] + got_b[0]).T
    else:
        half = rows // 2
        rows_ref[:half, :] = keep_a[...] + got_a[...]
        rows_ref[half:, :] = keep_b[...] + got_b[...]
    for m in range(count):
        rect_ref[pl.ds(pl.multiple_of((me ^ m) * each, each), each), :] = pieces[m][...]
    for i, block, low in strips(nb):
        wide = (block + 1) * BLOCK
        part = rect_ref[i * BLOCK : (i + 1) * BLOCK, low : low + wide]
        part = jnp.concatenate(
            [part[:, : wide - BLOCK], jnp.where(
                lax.broadcasted_iota(jnp.int32, (BLOCK, BLOCK), 1) <= lax.broadcasted_iota(jnp.int32, (BLOCK, BLOCK), 0),
                part[:, wide - BLOCK :], 0.0)], axis=1) if wide > BLOCK else part
        out_ref[:, block * BLOCK : (block + 1) * BLOCK] = three(split(rows_ref[:, :wide]), split(part), ((1,), (1,)))

    @pl.when(first < width)
    def _():
        out_ref[...] = own_ref[...]


def last(place, pieces, sums, own):
    rows, width = own.shape
    nb = width // BLOCK
    tall, wide = nb // 2 * BLOCK, (nb + 1) * BLOCK
    return pl.pallas_call(
        functools.partial(last_kernel, len(pieces)),
        out_shape=shape(rows, width),
        in_specs=[SMEM] + vmem(len(pieces) + 5),
        out_specs=vmem(1)[0],
        scratch_shapes=[pltpu.VMEM((tall, wide), jnp.float32), pltpu.VMEM((rows, width), jnp.float32)],
        compiler_params=pltpu.CompilerParams(vmem_limit_bytes=12 << 20),
        cost_estimate=pl.CostEstimate(flops=6 * rows * width * width, bytes_accessed=8 * width * width, transcendentals=0),
    )(place, *pieces, *sums, own)


def hop(x, source, target):
    return lax.ppermute(x, "col", [(source, target)])


def exchange(x, mask, count):
    return lax.ppermute(x, "scen", [(i, i ^ mask) for i in range(count)])


def orders(count):
    bits = count.bit_length() - 1
    split = 1 + bits // 2
    return bits, list(range(1, split)), list(range(split, bits))


def halve(x, names, bit, count):
    axis = names.index(bit)
    mine = (lax.axis_index("scen") >> bit) & 1
    keep = lax.dynamic_index_in_dim(x, mine, axis, keepdims=False)
    send = lax.dynamic_index_in_dim(x, 1 - mine, axis, keepdims=False)
    return keep, exchange(send, 1 << bit, count), [n for n in names if n != bit]


def scatter_sum(x):
    count = lax.axis_size("scen")
    bits, first, second = orders(count)
    rows = x.shape[0] // count
    x = x.reshape((2,) * bits + (rows,) + x.shape[1:])
    keep, got, names = halve(x, list(range(bits - 1, -1, -1)), 0, count)
    x = keep + got
    lead = (slice(None),) * len(names)
    parts = [x[lead + (slice(0, rows // 2),)], x[lead + (slice(rows // 2, rows),)]]
    lists, pairs = [names, names], [None, None]
    for a, b in zip(first + second, second + first):
        for i, bit in ((0, a), (1, b)):
            if pairs[i] is not None:
                parts[i] = pairs[i][0] + pairs[i][1]
            keep, got, lists[i] = halve(parts[i], lists[i], bit, count)
            pairs[i] = (keep, got)
    return pairs[0] + pairs[1]


def scatter_sum_columns(place, first, local, pieces):
    count = lax.axis_size("scen")
    bits, near, far = orders(count)
    half = first.shape[0] // 2
    keep, send = part(place, first, local, pieces, count)
    got = exchange(send, 1, count)
    left = [list(range(1, bits)), list(range(1, bits))]
    pairs = None
    for a, b in zip(near + far, far + near):
        if pairs is None:
            cuts = tuple((i * half, (i + 1) * half, left[i].index(bit), bit) for i, bit in ((0, a), (1, b)))
            outs = turn(place, keep, got, cuts)
        else:
            outs = ()
            for i, bit in ((0, a), (1, b)):
                outs += turn(place, *pairs[i], ((0, half, left[i].index(bit), bit),))
        pairs = []
        for i, bit in ((0, a), (1, b)):
            left[i].remove(bit)
            pairs.append((outs[2 * i], exchange(outs[2 * i + 1], 1 << bit, count)))
    return pairs[0] + pairs[1]


PIECES = 8
LATE = 1
HEAD = 2


def bounds(depth):
    units = depth // (2 * SUB)
    return [units * k // PIECES * 2 * SUB for k in range(PIECES + 1)]


def program(inverses, coupling, tile_mask, hess_diag):
    local = coupling[0]
    width = hess_diag.shape[0]
    scen, planes = lax.axis_size("scen"), lax.axis_size("col")
    me, plane = lax.axis_index("scen").astype(jnp.int32), lax.axis_index("col").astype(jnp.int32)
    rows = local.shape[1] // scen
    place = jnp.stack([plane, me, plane * local.shape[1] + me * rows])
    edge = bounds(local.shape[0])

    given = (place, tile_mask, inverses[0], local, width, edge)
    own = list(product(*given, 0, edge[HEAD], []))
    *more, keep_a, keep_b, send = product(*given, edge[HEAD], edge[-1], own)
    own += more

    groups = [own]
    for h in range(planes - 1):
        groups.append([hop(groups[h][k], h, h + 1) for k in range(PIECES)])

    got = exchange(send, 1, scen)
    a, b = keep_a + got[: got.shape[0] // 2], keep_b + got[got.shape[0] // 2 :]
    _, near, far = orders(scen)
    for p, q in zip(near + far, far + near):
        got_a = exchange(a, 1 << p, scen)
        got_b = exchange(b, 1 << q, scen)
        a, b = a + got_a, b + got_b
    parts = (a, b, exchange(a, 1, scen), exchange(b, 1, scen))
    each = width // BLOCK // 2 * BLOCK // scen
    lower, piece = factor(place, parts, hess_diag[None, :], each, rows)

    mine = jnp.where(plane == 0, piece, 0.0)
    for h in range(1, planes):
        piece = hop(piece, h - 1, h)
        mine = mine + piece
    pieces = [mine if m == 0 else exchange(mine, m, scen) for m in range(0, scen, 2)]
    pieces = [p for m in range(0, scen, 2) for p in (pieces[m // 2], exchange(pieces[m // 2], 1, scen))]

    cut = PIECES - LATE
    early = edge[cut]
    top = collect(place, [group[:cut] for group in groups])
    if rows % BLOCK == 0:
        first = high(top, local[:early], ((0,), (0,)))
        sums = scatter_sum_columns(place, first, local, [group[cut] for group in groups])
    else:
        bottom = collect(place, [group[cut:] for group in groups])
        first, second = high(local[:early], top, ((0,), (0,))), high(local[early:], bottom, ((0,), (0,)))
        sums = scatter_sum(first + second)
    return last(place, pieces, sums, lower)


def solution(mesh):
    in_specs = (P("scen", None, None), P("scen", None, "col"), P("scen", None), P())
    out_specs = P(("col", "scen"), None)
    return jax.shard_map(program, mesh=mesh, in_specs=in_specs, out_specs=out_specs, check_vma=False)
```
